32 devices in a mesh: layer: 2 (over core), rows: 16 (over z, y, x).
Axes of the slice: x: 2, y: 2, z: 4, core: 2. Of those that a mesh axis runs over, the one named last changes fastest.
Arguments:
- frames: bfloat16 [3, 32, 256, 256], P(None, 'rows'), may hold values from -6 to 6
- initial_state: bfloat16 [2, 32, 256, 256], P('layer', 'rows'), may hold values from -3 to 3
- w_gates: bfloat16 [2, 3, 3, 512, 512], P('layer'), may hold values from -0.25 to 0.25
- w_cand: bfloat16 [2, 3, 3, 512, 256], P('layer'), may hold values from -0.125 to 0.125
- biases: float32 [2, 768], P('layer'), may hold values from -4 to 4
Outputs:
- hidden_frames: bfloat16 [2, 3, 32, 256, 256], P('layer', None, 'rows')
The draws below stay inside these ranges and needn't reach their ends.
All inputs are finite; a program needn't handle non-finite values.
Results may differ from the reference program's by a relative error of at most 0.0048.
Values may be sent and summed in bfloat16 or wider, within the bound.
A program may use at most 64 MiB of HBM per device.

```python
import jax
import jax.numpy as jnp

CH = 256
COLS = 256
FRAMES = 3
LAYERS = 2
GRID_ROWS = 32


def block_scale(key, dims, cuts, low, largest):
    def one(position, shards_of):
        draws = jax.random.uniform(jax.random.fold_in(jax.random.fold_in(key, 6), position), (shards_of,), jnp.float32, low / len(cuts), largest / len(cuts))
        return jnp.repeat(jnp.exp(draws), dims[position] // shards_of).reshape((-1,) + (1,) * (len(dims) - position - 1))

    factor_of = one(*cuts[0])
    for cut in cuts[1:]:
        factor_of = factor_of * one(*cut)
    return factor_of


def normal_values(rng, extent, width, limit, cuts=(), held_as=jnp.bfloat16):
    values = width * jax.random.normal(rng, extent, jnp.float32)
    if cuts:
        values = values * block_scale(rng, extent, cuts, -0.22, 0.18)
    return jnp.clip(values, -limit, limit).astype(held_as)


def setup_inputs(seed: int = 0) -> dict:
    arg_keys = jax.random.split(jax.random.key(seed), 6)
    return {
        "frames": normal_values(arg_keys[0], (FRAMES, GRID_ROWS, COLS, CH), 1.0, 6.0, ((1, 16),)),
        "initial_state": normal_values(arg_keys[1], (LAYERS, GRID_ROWS, COLS, CH), 1.2, 3.0, ((0, 2), (1, 16))),
        "w_gates": normal_values(arg_keys[2], (LAYERS, 3, 3, 2 * CH, 2 * CH), (5 * CH // 2) ** -0.5, 0.25, ((0, 2),)),
        "w_cand": normal_values(arg_keys[3], (LAYERS, 3, 3, 2 * CH, CH), (9 * CH) ** -0.5, 0.125, ((0, 2),)),
        "biases": normal_values(arg_keys[4], (LAYERS, 3 * CH), 1.0, 4.0, ((0, 2),), jnp.float32),
    }


def convolve(source_rows, weight):
    row_count, col_count, _ = source_rows.shape
    padded = jnp.pad(source_rows, ((1, 1), (1, 1), (0, 0)))
    summed = jnp.zeros((row_count * col_count, weight.shape[3]), jnp.float32)
    for row_off in range(3):
        for col_off in range(3):
            tap_view = padded[row_off:row_off + row_count, col_off:col_off + col_count].reshape(row_count * col_count, -1)
            summed = summed + jnp.dot(tap_view, weight[row_off, col_off], preferred_element_type=jnp.float32)
    return summed.reshape(row_count, col_count, -1)


def reference(frames, initial_state, w_gates, w_cand, biases):
    channels = initial_state.shape[-1]
    sequence = frames
    collected = []
    for layer_idx in range(LAYERS):
        hidden = initial_state[layer_idx]
        produced = []
        for frame_idx in range(FRAMES):
            inputs = sequence[frame_idx]
            gate_pre = convolve(jnp.concatenate([inputs, hidden], -1), w_gates[layer_idx]) + biases[layer_idx, :2 * channels]
            gate_all = jax.nn.sigmoid(gate_pre)
            update = gate_all[..., :channels]
            reset_gate = gate_all[..., channels:]
            reset_state = (reset_gate * hidden.astype(jnp.float32)).astype(jnp.bfloat16)
            candidate = jnp.tanh(convolve(jnp.concatenate([inputs, reset_state], -1), w_cand[layer_idx]) + biases[layer_idx, 2 * channels:])
            hidden = ((1.0 - update) * hidden.astype(jnp.float32) + update * candidate).astype(jnp.bfloat16)
            produced.append(hidden)
        sequence = jnp.stack(produced)
        collected.append(sequence)
    return jnp.stack(collected)
```

```python
import functools

import jax
import jax.numpy as jnp
from jax import lax
from jax.experimental import pallas as pl
from jax.experimental.pallas import tpu as pltpu
from jax.sharding import PartitionSpec as P

MESH = pl.DeviceIdType.MESH

ROW_DIRS = ((-1, 0), (1, 0))
COL_DIRS = ((0, -1), (0, 1), (-1, -1), (-1, 1), (1, -1), (1, 1))
DIRS = ROW_DIRS + COL_DIRS


def reorder(c, group):
    if group == 4:
        return c + (c // 2) * (5 - 2 * c)
    return c


def sigmoid(v):
    return 0.5 * jnp.tanh(0.5 * v) + 0.5


def kernel(
    count, group, frames_ref, init_ref, wg_ref, wc_ref, bias_ref, out_ref,
    wg, wc, fields, cols, stage, stage32, strips, im_x, ime_x, im_h, ime_h, edge,
    rx, ux, cx, rh, uh, rs, im_rs, rs_edge,
    w_sem, own_sem, init_send, init_recv, x_send, x_recv, pass_send, pass_recv,
    out_own, out_send, out_recv, halo_send, halo_recv,
):
    frame_count, strip, all_cols, ch = frames_ref.shape
    height = strip * group
    width = all_cols // group
    tile = height * width
    ring = (height + 2) * width
    pad = ime_x.shape[0] // 2
    layer = lax.axis_index("layer")
    last_layer = lax.axis_size("layer") - 1
    index = lax.axis_index("rows")
    planes = count // group
    q = index // group
    c = index % group
    t = reorder(c, group)
    first_x = frame_count + 1
    f32, bf16 = jnp.float32, jnp.bfloat16
    both = jnp.logical_and

    def exists(step_row, step_col):
        terms = []
        if step_row < 0:
            terms.append(q > 0)
        if step_row > 0:
            terms.append(q < planes - 1)
        if step_col < 0:
            terms.append(t > 0)
        if step_col > 0:
            terms.append(t < group - 1)
        return functools.reduce(jnp.logical_and, terms)

    def at(step_row, step_col, hop=0):
        rows = (q + step_row) * group + reorder(t + step_col, group)
        return {"layer": layer + hop, "rows": rows}

    copy_wg = pltpu.make_async_copy(wg_ref, wg, w_sem.at[0])
    copy_wc = pltpu.make_async_copy(wc_ref, wc, w_sem.at[1])
    own_cols = pl.ds(pl.multiple_of(t * width, width), width)
    own_rows = pl.ds(2 + c * strip, strip)
    inner = pl.ds(2, height)

    def own_init():
        return pltpu.make_async_copy(
            init_ref.at[:, own_cols, :], fields.at[0, own_rows], own_sem.at[0]
        )

    def own_frame(f):
        return pltpu.make_async_copy(
            frames_ref.at[f, :, own_cols, :], fields.at[first_x + f, own_rows], own_sem.at[1 + f]
        )

    def member(d):
        return lax.rem(c + d, group)

    def init_copy(d):
        target = member(d)
        tcols = pl.ds(pl.multiple_of(reorder(target, group) * width, width), width)
        return pltpu.make_async_remote_copy(
            src_ref=init_ref.at[:, tcols, :], dst_ref=fields.at[0, own_rows],
            send_sem=init_send.at[d], recv_sem=init_recv.at[d],
            device_id={"rows": q * group + target}, device_id_type=MESH,
        )

    def frame_copy(f, d):
        target = member(d)
        tcols = pl.ds(pl.multiple_of(reorder(target, group) * width, width), width)
        return pltpu.make_async_remote_copy(
            src_ref=frames_ref.at[f, :, tcols, :], dst_ref=fields.at[first_x + f, own_rows],
            send_sem=x_send.at[f, d], recv_sem=x_recv.at[f, d],
            device_id={"rows": q * group + target}, device_id_type=MESH,
        )

    def start_frame(f):
        own_frame(f).start()
        for d in range(1, group):
            frame_copy(f, d).start()

    def wait_frame(f):
        own_frame(f).wait()
        for d in range(1, group):
            frame_copy(f, d).wait_recv()

    def pass_copy(f):
        return pltpu.make_async_remote_copy(
            src_ref=fields.at[f + 1, inner], dst_ref=fields.at[first_x + f, inner],
            send_sem=pass_send.at[f], recv_sem=pass_recv.at[f],
            device_id={"layer": jnp.minimum(layer + 1, last_layer)}, device_id_type=MESH,
        )

    def out_copy(f, d):
        target = member(d)
        return pltpu.make_async_remote_copy(
            src_ref=fields.at[f + 1, pl.ds(2 + target * strip, strip)],
            dst_ref=out_ref.at[0, f, :, own_cols, :],
            send_sem=out_send.at[f, d], recv_sem=out_recv.at[f, d],
            device_id={"rows": q * group + target}, device_id_type=MESH,
        )

    def own_out(f):
        return pltpu.make_async_copy(
            fields.at[f + 1, own_rows], out_ref.at[0, f, :, own_cols, :], out_own.at[f]
        )

    def send_out(f):
        for d in range(1, group):
            out_copy(f, d).start()
        own_out(f).start()

    def halo_copy(src, dst, k, hop):
        dr, dc = DIRS[k]
        back = DIRS.index((-dr, -dc))
        if dc == 0:
            src_ref = fields.at[src, pl.ds(2, 2) if dr < 0 else pl.ds(height, 2)]
            dst_ref = fields.at[dst, pl.ds(height + 2, 2) if dr < 0 else pl.ds(0, 2)]
        else:
            src_ref = stage.at[src, 0 if dc < 0 else 1]
            dst_ref = cols.at[dst, back - 2]
        return pltpu.make_async_remote_copy(
            src_ref=src_ref, dst_ref=dst_ref,
            send_sem=halo_send.at[hop, src, k], recv_sem=halo_recv.at[dst, back],
            device_id=at(dr, dc, hop), device_id_type=MESH,
        )

    def halo_arrival(dst, k):
        dr, dc = DIRS[k]
        if dc == 0:
            ref = fields.at[dst, pl.ds(0, 2) if dr < 0 else pl.ds(height + 2, 2)]
        else:
            ref = cols.at[dst, k - 2]
        return pltpu.make_async_remote_copy(
            src_ref=ref, dst_ref=ref,
            send_sem=halo_send.at[0, dst, k], recv_sem=halo_recv.at[dst, k],
            device_id=at(dr, dc), device_id_type=MESH,
        )

    def each(action):
        for k, (dr, dc) in enumerate(DIRS):
            pl.when(exists(dr, dc))(functools.partial(action, k))

    def send_halo(src, dst, hop):
        each(lambda k: halo_copy(src, dst, k, hop).start())

    def sent_halo(src, dst, hop):
        each(lambda k: halo_copy(src, dst, k, hop).wait_send())

    def wait_halo(dst):
        each(lambda k: halo_arrival(dst, k).wait_recv())

    copy_wg.start()
    copy_wc.start()
    own_init().start()

    barrier = pltpu.get_barrier_semaphore()
    greeted = []
    for d in range(1, group):
        greeted.append((None, {"rows": q * group + member(d)}))
    for dr, dc in DIRS:
        if dr != 0:
            greeted.append((exists(dr, dc), at(dr, dc)))
    for hop in (-1, 1):
        near = layer > 0 if hop < 0 else layer < last_layer
        greeted.append((near, {"layer": layer + hop}))
        for dr, dc in DIRS:
            greeted.append((both(near, exists(dr, dc)), at(dr, dc, hop)))
    expected = 0
    for cond, where in greeted:
        def greet(where=where):
            pl.semaphore_signal(barrier, inc=1, device_id=where, device_id_type=MESH)

        if cond is None:
            greet()
            expected = expected + 1
        else:
            pl.when(cond)(greet)
            expected = expected + jnp.where(cond, 1, 0)
    pl.semaphore_wait(barrier, expected)

    for d in range(1, group):
        init_copy(d).start()
    pl.when(layer == 0)(lambda: start_frame(0))

    for k, (dr, dc) in enumerate(DIRS):
        @pl.when(jnp.logical_not(exists(dr, dc)))
        def _(k=k, dr=dr, dc=dc):
            def clear(g, carry):
                if dc == 0:
                    rows = pl.ds(0, 2) if dr < 0 else pl.ds(height + 2, 2)
                    fields[g, rows] = jnp.zeros((2, width, ch), bf16)
                else:
                    cols[g, k - 2] = jnp.zeros((2 * height, ch), bf16)
                return carry

            lax.fori_loop(0, 2 * frame_count + 1, clear, 0)

    strips[...] = jnp.zeros_like(strips)

    first_col = lax.broadcasted_iota(jnp.int32, (width, ch), 0) == 0
    last_col = lax.broadcasted_iota(jnp.int32, (width, ch), 0) == width - 1

    def stage_row(i, first, last):
        for s, v in enumerate((first, last)):
            for k in range(2):
                lo = k if s == 0 else v.shape[0] - 2 + k
                stage32[s, k * height + i : k * height + i + 1, :] = v[lo : lo + 1]

    def stage_done(g):
        stage[g] = stage32[...].astype(bf16)

    def stage_field(g):
        for i in range(height):
            stage_row(
                i,
                fields[g, 2 + i, 0:16, :].astype(f32),
                fields[g, 2 + i, width - 16 : width, :].astype(f32),
            )
        stage_done(g)

    def shifted(v, left, right):
        before = jnp.where(first_col, jnp.broadcast_to(left, v.shape), pltpu.roll(v, 1, 0))
        after = jnp.where(
            last_col, jnp.broadcast_to(right, v.shape), pltpu.roll(v, width - 1, 0)
        )
        return before.astype(bf16), after.astype(bf16)

    def gather(g, im, ime, keep_edge):
        for s in range(2):
            for part, k in enumerate((2 + s, s, 4 + s)):
                v = cols[g, k].astype(f32)
                for j in range(2):
                    strips[4 * s + j, part * height : (part + 1) * height, :] = (
                        v[j * height : (j + 1) * height]
                    )
        for j in range(height + 4):
            v = fields[g, j].astype(f32)
            r = height + j - 2
            strips[2, r : r + 1, :] = v[0:1]
            strips[3, r : r + 1, :] = v[width - 1 : width]
            before, after = shifted(v, strips[1, r : r + 1, :], strips[4, r : r + 1, :])
            im[j * width : (j + 1) * width, 0:ch] = before
            im[j * width : (j + 1) * width, ch : 2 * ch] = after
        for a in range(3):
            for b in range(3):
                lo = height - 2 + a
                lanes = slice((a * 3 + b) * ch, (a * 3 + b + 1) * ch)
                ime[0:pad, lanes] = strips[b, lo : lo + pad, :].astype(bf16)
                ime[pad : 2 * pad, lanes] = strips[3 + b, lo : lo + pad, :].astype(bf16)
        if keep_edge:
            edge[0:pad, :] = strips[1, height - 1 : height - 1 + pad, :]
            edge[pad : 2 * pad, :] = strips[4, height - 1 : height - 1 + pad, :]

    def conv(center, im, ime, row, rows, weight, base, lo):
        left, right = [], []
        for a in range(3):
            for b in range(3):
                j = row + a
                if b == 1:
                    piece = center(j, rows).reshape(rows * width, ch)
                else:
                    piece = im[j * width : (j + rows) * width, (b // 2) * ch : (b // 2 + 1) * ch]
                if ime is not None:
                    lanes = slice((a * 3 + b) * ch, (a * 3 + b + 1) * ch)
                    piece = jnp.concatenate([piece, ime[:, lanes]], axis=0)
                left.append(piece)
                k = b * 2 * ch + base
                right.append(weight[a, k : k + ch, lo : lo + ch])
        return jnp.dot(
            jnp.concatenate(left, axis=1), jnp.concatenate(right, axis=0),
            preferred_element_type=f32,
        )

    def input_part(f):
        g = first_x + f
        center = lambda j, rows: fields[g, j : j + rows]
        gather(g, im_x, ime_x, False)
        rx[...] = conv(center, im_x, ime_x, 0, height + 2, wg, 0, ch) + bias_ref[:, ch : 2 * ch]
        ux[...] = conv(center, im_x, None, 1, height, wg, 0, 0) + bias_ref[:, 0:ch]
        cx[...] = conv(center, im_x, None, 1, height, wc, 0, 0) + bias_ref[:, 2 * ch : 3 * ch]

    def state_part(f):
        center = lambda j, rows: fields[f, j : j + rows]
        gather(f, im_h, ime_h, True)
        rh[...] = conv(center, im_h, ime_h, 0, height + 2, wg, ch, ch)
        uh[...] = conv(center, im_h, None, 1, height, wg, ch, 0)

    def update_state(f):
        rs_edge[...] = sigmoid(rx[ring:, :] + rh[ring:, :]) * edge[...]
        for j in range(height + 2):
            rows = slice(j * width, (j + 1) * width)
            v = sigmoid(rx[rows, :] + rh[rows, :]) * fields[f, 1 + j].astype(f32)
            rs[j] = v.astype(bf16)
            before, after = shifted(v, rs_edge[j : j + 1, :], rs_edge[pad + j : pad + j + 1, :])
            im_rs[rows, 0:ch] = before
            im_rs[rows, ch : 2 * ch] = after
        center = lambda j, rows: rs[j : j + rows]
        inside = conv(center, im_rs, None, 0, height, wc, ch, 0)
        for i in range(height):
            rows = slice(i * width, (i + 1) * width)
            update = sigmoid(ux[rows, :] + uh[rows, :])
            candidate = jnp.tanh(cx[rows, :] + inside[rows])
            fresh = (1.0 - update) * fields[f, 2 + i].astype(f32) + update * candidate
            fields[f + 1, 2 + i] = fresh.astype(bf16)
            stage_row(i, fresh, fresh)
        stage_done(f + 1)

    own_init().wait()
    for d in range(1, group):
        init_copy(d).wait_recv()
    stage_field(0)
    send_halo(0, 0, 0)

    @pl.when(layer == 0)
    def _():
        wait_frame(0)
        stage_field(first_x)
        send_halo(first_x, first_x, 0)
        if frame_count > 1:
            start_frame(1)

    def step(f, carry):
        wait_halo(f)
        pl.when(f == 0)(lambda: copy_wg.wait())
        state_part(f)
        pl.when(f > 0)(lambda: send_out(f - 1))
        pl.when(f == 0)(lambda: copy_wc.wait())

        @pl.when(jnp.logical_or(layer > 0, f == 0))
        def _():
            pl.when(layer > 0)(lambda: pass_copy(f).wait_recv())
            wait_halo(first_x + f)
            input_part(f)

        @pl.when(both(layer == 0, f + 1 < frame_count))
        def _():
            wait_frame(f + 1)
            stage_field(first_x + f + 1)
            send_halo(first_x + f + 1, first_x + f + 1, 0)
            pl.when(f + 2 < frame_count)(lambda: start_frame(f + 2))

        update_state(f)
        pl.when(f + 1 < frame_count)(lambda: send_halo(f + 1, f + 1, 0))

        @pl.when(layer < last_layer)
        def _():
            pass_copy(f).start()
            send_halo(f + 1, first_x + f, 1)

        @pl.when(both(layer == 0, f + 1 < frame_count))
        def _():
            wait_halo(first_x + f + 1)
            input_part(f + 1)

        return carry

    lax.fori_loop(0, frame_count, step, 0)
    send_out(frame_count - 1)

    sent_halo(0, 0, 0)
    for d in range(1, group):
        init_copy(d).wait_send()

    def finish(f, carry):
        own_out(f).wait()
        for d in range(1, group):
            out_copy(f, d).wait()
        pl.when(f + 1 < frame_count)(lambda: sent_halo(f + 1, f + 1, 0))

        @pl.when(layer < last_layer)
        def _():
            pass_copy(f).wait_send()
            sent_halo(f + 1, first_x + f, 1)

        @pl.when(layer == 0)
        def _():
            sent_halo(first_x + f, first_x + f, 0)
            for d in range(1, group):
                frame_copy(f, d).wait_send()

        return carry

    lax.fori_loop(0, frame_count, finish, 0)


def shards(count, frames, initial_state, w_gates, w_cand, biases):
    frame_count, strip, cols, ch = frames.shape
    group = 4 if count % 4 == 0 else 1
    height, width = strip * group, cols // group
    dma = pltpu.SemaphoreType.DMA
    bf16, f32 = jnp.bfloat16, jnp.float32
    anywhere = pl.BlockSpec(memory_space=pltpu.HBM)
    rows_k = w_gates.shape[2] * w_gates.shape[3]
    tile = height * width
    ring = (height + 2) * width
    pad = -(-(height + 2) // 16) * 16
    held = 2 * frame_count + 1
    out = (1, frame_count, strip, cols, ch)
    return pl.pallas_call(
        functools.partial(kernel, count, group),
        out_shape=pltpu.VMEM(out, bf16),
        in_specs=[anywhere] * 4 + [pl.BlockSpec(memory_space=pltpu.VMEM)],
        out_specs=pl.BlockSpec(memory_space=pltpu.VMEM),
        scratch_shapes=[
            pltpu.VMEM((3, rows_k, 2 * ch), bf16),
            pltpu.VMEM((3, rows_k, ch), bf16),
            pltpu.VMEM((held, height + 4, width, ch), bf16),
            pltpu.VMEM((held, 6, 2 * height, ch), bf16),
            pltpu.VMEM((held, 2, 2 * height, ch), bf16),
            pltpu.VMEM((2, 2 * height, ch), f32),
            pltpu.VMEM((6, 3 * height, ch), f32),
            pltpu.VMEM(((height + 4) * width, 2 * ch), bf16),
            pltpu.VMEM((2 * pad, 9 * ch), bf16),
            pltpu.VMEM(((height + 4) * width, 2 * ch), bf16),
            pltpu.VMEM((2 * pad, 9 * ch), bf16),
            pltpu.VMEM((2 * pad, ch), f32),
            pltpu.VMEM((ring + 2 * pad, ch), f32),
            pltpu.VMEM((tile, ch), f32),
            pltpu.VMEM((tile, ch), f32),
            pltpu.VMEM((ring + 2 * pad, ch), f32),
            pltpu.VMEM((tile, ch), f32),
            pltpu.VMEM((height + 2, width, ch), bf16),
            pltpu.VMEM((ring, 2 * ch), bf16),
            pltpu.VMEM((2 * pad, ch), f32),
            dma((2,)), dma((1 + frame_count,)), dma((group,)), dma((group,)),
            dma((frame_count, group)), dma((frame_count, group)),
            dma((frame_count,)), dma((frame_count,)),
            dma((frame_count,)), dma((frame_count, group)), dma((frame_count, group)),
            dma((2, held, 8)), dma((held, 8)),
        ],
        compiler_params=pltpu.CompilerParams(
            collective_id=0, has_side_effects=True, vmem_limit_bytes=60_000_000
        ),
    )(
        frames,
        initial_state[0],
        w_gates.reshape(3, rows_k, 2 * ch),
        w_cand.reshape(3, rows_k, ch),
        biases,
    )


def solution(mesh):
    placed = (
        P(None, "rows", None, None),
        P("layer", "rows", None, None),
        P("layer", None, None, None, None),
        P("layer", None, None, None, None),
        P("layer", None),
    )
    return jax.shard_map(
        functools.partial(shards, mesh.shape["rows"]),
        mesh=mesh,
        in_specs=placed,
        out_specs=P("layer", None, "rows", None, None),
        check_vma=False,
    )
```

```python
import functools

import jax
import jax.numpy as jnp
from jax import lax
from jax.experimental import pallas as pl
from jax.experimental.pallas import tpu as pltpu
from jax.sharding import PartitionSpec as P

MESH = pl.DeviceIdType.MESH

ROW_DIRS = ((-1, 0), (1, 0))
COL_DIRS = ((0, -1), (0, 1), (-1, -1), (-1, 1), (1, -1), (1, 1))
DIRS = ROW_DIRS + COL_DIRS


def reorder(c, group):
    if group == 4:
        return c + (c // 2) * (5 - 2 * c)
    return c


def sigmoid(v):
    return 0.5 * jnp.tanh(0.5 * v) + 0.5


def kernel(
    count, group, frames_ref, init_ref, wg_ref, wc_ref, bias_ref, out_ref,
    wg, wc, own, packs, packs32, packed, fields, cols, stage, stage32,
    strips_x, strips_h, im_x, ime_x, im_h, ime_h, edge,
    rx, ux, cx, rh, uh, rs, im_rs, rs_edge, span,
    w_sem, load_sem, push_send, push_recv, pass_send, pass_recv,
    out_own, out_send, out_recv, halo_send, halo_recv,
):
    frame_count, strip, all_cols, ch = frames_ref.shape
    height = strip * group
    width = all_cols // group
    tile = height * width
    ring = (height + 2) * width
    pad = ime_x.shape[0] // 2
    layer = lax.axis_index("layer")
    last_layer = lax.axis_size("layer") - 1
    index = lax.axis_index("rows")
    planes = count // group
    q = index // group
    c = index % group
    t = reorder(c, group)
    first_x = frame_count + 1
    f32, bf16 = jnp.float32, jnp.bfloat16
    both = jnp.logical_and
    one = lambda cond: jnp.where(cond, 1, 0)

    def exists(step_row, step_col):
        terms = []
        if step_row < 0:
            terms.append(q > 0)
        if step_row > 0:
            terms.append(q < planes - 1)
        if step_col < 0:
            terms.append(t > 0)
        if step_col > 0:
            terms.append(t < group - 1)
        return functools.reduce(jnp.logical_and, terms)

    def at(step_row, step_col, hop=0):
        rows = (q + step_row) * group + reorder(t + step_col, group)
        return {"layer": layer + hop, "rows": rows}

    def member(d):
        return lax.rem(c + d, group)

    def send(src, dst, send_sem, recv_sem, where):
        return pltpu.make_async_remote_copy(
            src_ref=src, dst_ref=dst, send_sem=send_sem, recv_sem=recv_sem,
            device_id=where, device_id_type=MESH,
        )

    def drain(pixels, send_sem=None, recv_sem=None):
        part = span.at[pl.ds(0, pixels)]
        sem = recv_sem if send_sem is None else send_sem
        copy = send(part, part, sem, sem, {"layer": last_layer - layer})
        copy.wait_recv() if send_sem is None else copy.wait_send()

    copy_wg = pltpu.make_async_copy(wg_ref, wg, w_sem.at[0])
    copy_wc = pltpu.make_async_copy(wc_ref, wc, w_sem.at[1])
    own_cols = pl.ds(pl.multiple_of(t * width, width), width)
    own_rows = pl.ds(2 + c * strip, strip)
    inner = pl.ds(2, height)
    above, below = pl.ds(0, 2), pl.ds(height + 2, 2)

    def load(k):
        src = init_ref if k == 0 else frames_ref.at[k - 1]
        return pltpu.make_async_copy(src, own.at[k], load_sem.at[k])

    def place_own():
        return pltpu.make_async_copy(
            own.at[0, :, own_cols, :], fields.at[0, own_rows], load_sem.at[1 + frame_count]
        )

    def push(k, to_layer, skip_self):
        g = 0 if k == 0 else first_x + k - 1
        for d in range(1 if skip_self else 0, group):
            target = member(d)
            place = reorder(target, group)
            tcols = pl.ds(pl.multiple_of(place * width, width), width)
            where = {"layer": to_layer, "rows": q * group + target}
            sems = push_send.at[0, k], push_recv.at[0, k]
            send(own.at[k, :, tcols, :], fields.at[g, own_rows], *sems, where).start()
            send(packs.at[k, place], packed.at[k, c], *sems, where).start()
        for step, edge_strip, src, dst, slot in (
            (-1, 0, pl.ds(0, 2), below, group + 1), (1, group - 1, pl.ds(strip - 2, 2), above, group)
        ):
            @pl.when(both(c == edge_strip, exists(step, 0)))
            def _(step=step, src=src, dst=dst, slot=slot):
                sems = push_send.at[1, k], push_recv.at[1, k]
                for place in range(group):
                    tcols = pl.ds(place * width, width)
                    where = {"layer": to_layer, "rows": (q + step) * group + reorder(place, group)}
                    send(own.at[k, src, tcols, :], fields.at[g, dst], *sems, where).start()
                    send(packs.at[k, place], packed.at[k, slot], *sems, where).start()

    pack_rows = packs.shape[2]
    pushed = strip * width + pack_rows

    def sent_push(k, skip_self):
        drain((group - 1 if skip_self else group) * pushed, send_sem=push_send.at[0, k])
        for step, edge_strip in ((-1, 0), (1, group - 1)):
            @pl.when(both(c == edge_strip, exists(step, 0)))
            def _():
                drain(group * pushed, send_sem=push_send.at[1, k])

    def wait_plane(k, skip_self):
        drain((group - 1 if skip_self else group) * pushed, recv_sem=push_recv.at[0, k])

    def wait_vertical(k):
        for n in (1, 2):
            @pl.when(one(q > 0) + one(q < planes - 1) == n)
            def _(n=n):
                drain(n * pushed, recv_sem=push_recv.at[1, k])

    def pass_copy(f):
        return send(
            fields.at[f + 1, inner], fields.at[first_x + f, inner],
            pass_send.at[f], pass_recv.at[f], {"layer": jnp.minimum(layer + 1, last_layer)},
        )

    def own_out(f):
        return pltpu.make_async_copy(
            fields.at[f + 1, own_rows], out_ref.at[0, f, :, own_cols, :], out_own.at[f]
        )

    def send_out(f):
        for d in range(group - 1, 0, -1):
            target = member(d)
            send(
                fields.at[f + 1, pl.ds(2 + target * strip, strip)],
                out_ref.at[0, f, :, own_cols, :],
                out_send.at[f], out_recv.at[f], {"rows": q * group + target},
            ).start()
        own_out(f).start()

    def halo_copy(src, dst, k, hop):
        dr, dc = DIRS[k]
        back = DIRS.index((-dr, -dc))
        if dc == 0:
            src_ref = fields.at[src, pl.ds(2, 2) if dr < 0 else pl.ds(height, 2)]
            dst_ref = fields.at[dst, below if dr < 0 else above]
        else:
            src_ref = stage.at[src, 0 if dc < 0 else 1]
            dst_ref = cols.at[dst, back - 2]
        return send(
            src_ref, dst_ref, halo_send.at[hop, src], halo_recv.at[dst], at(dr, dc, hop)
        )

    def send_halo(src, dst, hop):
        for k, (dr, dc) in enumerate(DIRS):
            pl.when(exists(dr, dc))(lambda k=k: halo_copy(src, dst, k, hop).start())

    def drain_halo(**sem):
        upright = one(q > 0) + one(q < planes - 1)
        sideways = one(t > 0) + one(t < group - 1)
        for u in range(3):
            for s in range(3):
                pixels = u * 2 * width + s * (1 + u) * 2 * height
                if pixels:
                    @pl.when(both(upright == u, sideways == s))
                    def _(pixels=pixels):
                        drain(pixels, **sem)

    def sent_halo(src, hop):
        drain_halo(send_sem=halo_send.at[hop, src])

    def wait_halo(dst):
        drain_halo(recv_sem=halo_recv.at[dst])

    load(0).start()

    @pl.when(layer == last_layer)
    def _():
        for k in range(1, 1 + frame_count):
            load(k).start()

    copy_wg.start()
    copy_wc.start()

    barrier = pltpu.get_barrier_semaphore()
    expected = (group - 1) + group * last_layer
    for hop in range(2):
        where_layer = layer if hop == 0 else last_layer - layer
        for d in range(0 if hop else 1, group):
            pl.semaphore_signal(
                barrier, inc=1, device_id={"layer": where_layer, "rows": q * group + member(d)},
                device_id_type=MESH,
            )
        for step in (-1, 1):
            @pl.when(exists(step, 0))
            def _(step=step, where_layer=where_layer):
                for place in range(group):
                    pl.semaphore_signal(
                        barrier, inc=1,
                        device_id={"layer": where_layer, "rows": (q + step) * group + place},
                        device_id_type=MESH,
                    )

            expected = expected + group * one(exists(step, 0))

    for dr, dc in ROW_DIRS:
        @pl.when(jnp.logical_not(exists(dr, dc)))
        def _(dr=dr):
            def clear(g, carry):
                fields[g, above if dr < 0 else below] = jnp.zeros((2, width, ch), bf16)
                return carry

            lax.fori_loop(0, 2 * frame_count + 1, clear, 0)
            for k in range(1 + frame_count):
                packed[k, group if dr < 0 else group + 1] = jnp.zeros((pack_rows, ch), bf16)

    for k, (dr, dc) in enumerate(COL_DIRS):
        @pl.when(jnp.logical_not(exists(dr, dc)))
        def _(k=k):
            def clear(g, carry):
                cols[g, k] = jnp.zeros((2 * height, ch), bf16)
                return carry

            lax.fori_loop(1, 2 * frame_count + 1, clear, 0)

    strips_x[...] = jnp.zeros_like(strips_x)
    strips_h[...] = jnp.zeros_like(strips_h)
    packs32[...] = jnp.zeros_like(packs32)

    def make_packs(k):
        for place in range(group):
            for r in range(strip):
                lo, hi = place * width, (place + 1) * width
                if place > 0:
                    v = own[k, r, lo - 16 : lo, :].astype(f32)
                    packs32[place, r : r + 1, :] = v[14:15]
                    packs32[place, strip + r : strip + r + 1, :] = v[15:16]
                if place < group - 1:
                    v = own[k, r, hi : hi + 16, :].astype(f32)
                    packs32[place, 2 * strip + r : 2 * strip + r + 1, :] = v[0:1]
                    packs32[place, 3 * strip + r : 3 * strip + r + 1, :] = v[1:2]
        packs[k] = packs32[...].astype(bf16)

    load(0).wait()
    make_packs(0)
    packed[0, c] = packs[0, t]

    @pl.when(layer == last_layer)
    def _():
        for k in range(1, 1 + frame_count):
            load(k).wait()
            make_packs(k)

    pl.semaphore_wait(barrier, expected)
    place_own().start()

    @pl.when(layer < last_layer)
    def _():
        push(0, layer, True)

    @pl.when(layer == last_layer)
    def _():
        push(1, 0, False)
        sent_push(1, False)
        push(0, layer, True)
        sent_push(0, True)
        for k in range(2, 1 + frame_count):
            push(k, 0, False)

    first_col = lax.broadcasted_iota(jnp.int32, (width, ch), 0) == 0
    last_col = lax.broadcasted_iota(jnp.int32, (width, ch), 0) == width - 1

    def stage_row(i, v):
        for s, lo in enumerate((0, width - 2)):
            for k in range(2):
                stage32[s, k * height + i : k * height + i + 1, :] = v[lo + k : lo + k + 1]

    def shifted(v, left, right):
        before = jnp.where(first_col, jnp.broadcast_to(left, v.shape), pltpu.roll(v, 1, 0))
        after = jnp.where(
            last_col, jnp.broadcast_to(right, v.shape), pltpu.roll(v, width - 1, 0)
        )
        return before.astype(bf16), after.astype(bf16)

    sides = (0, 1, 4, 5)

    def fill(strips, k, slot, row):
        v = packed[k, slot].astype(f32)
        for j, s in enumerate(sides):
            strips[s, row : row + strip, :] = v[j * strip : (j + 1) * strip]

    def fill_plane(strips, k):
        for m in range(group):
            fill(strips, k, m, height + m * strip)

    def fill_vertical(strips, k):
        fill(strips, k, group, height - strip)
        fill(strips, k, group + 1, 2 * height)

    def fill_halo(strips, g):
        for s in range(2):
            for part, k in enumerate((2 + s, s, 4 + s)):
                v = cols[g, k].astype(f32)
                for j in range(2):
                    strips[4 * s + j, part * height : (part + 1) * height, :] = (
                        v[j * height : (j + 1) * height]
                    )

    def gather(g, strips, im, rows):
        for j in rows:
            v = fields[g, j].astype(f32)
            r = height + j - 2
            strips[2, r : r + 1, :] = v[0:1]
            strips[3, r : r + 1, :] = v[width - 1 : width]
            before, after = shifted(v, strips[1, r : r + 1, :], strips[4, r : r + 1, :])
            im[j * width : (j + 1) * width, 0:ch] = before
            im[j * width : (j + 1) * width, ch : 2 * ch] = after

    every_row = range(height + 4)
    middle_rows = range(2, height + 2)
    outer_rows = (0, 1, height + 2, height + 3)

    def gather_edge(strips, ime, keep):
        for a in range(3):
            for b in range(3):
                lo = height - 2 + a
                lanes = slice((a * 3 + b) * ch, (a * 3 + b + 1) * ch)
                ime[0:pad, lanes] = strips[b, lo : lo + pad, :].astype(bf16)
                ime[pad : 2 * pad, lanes] = strips[3 + b, lo : lo + pad, :].astype(bf16)
        if keep:
            edge[0:pad, :] = strips[1, height - 1 : height - 1 + pad, :]
            edge[pad : 2 * pad, :] = strips[4, height - 1 : height - 1 + pad, :]

    def taps(center, im, ime, blocks):
        for a in range(3):
            for b in range(3):
                pieces = []
                for row, rows in blocks:
                    j = row + a
                    if b == 1:
                        pieces.append(center(j, rows).reshape(rows * width, ch))
                    else:
                        lo = (b // 2) * ch
                        pieces.append(im[j * width : (j + rows) * width, lo : lo + ch])
                if ime is not None:
                    pieces.append(ime[:, (a * 3 + b) * ch : (a * 3 + b + 1) * ch])
                yield jnp.concatenate(pieces, axis=0) if len(pieces) > 1 else pieces[0]

    def kernels(weight, base, lo):
        return [
            weight[a, b * 2 * ch + base : b * 2 * ch + base + ch, lo : lo + ch]
            for a in range(3) for b in range(3)
        ]

    def dot(left, right):
        return jnp.dot(
            jnp.concatenate(left, axis=1), jnp.concatenate(right, axis=0),
            preferred_element_type=f32,
        )

    def x_taps(f, ime, blocks):
        g = first_x + f
        return list(taps(lambda j, rows: fields[g, j : j + rows], im_x, ime, blocks))

    def h_taps(f, ime, blocks):
        return list(taps(lambda j, rows: fields[f, j : j + rows], im_h, ime, blocks))

    whole_ring = ((0, height + 2),)
    whole_tile = ((1, height),)
    bias = lambda n: bias_ref[:, n * ch : (n + 1) * ch]

    def input_ring(f):
        rx[...] = dot(x_taps(f, ime_x, whole_ring), kernels(wg, 0, ch)) + bias(1)

    def input_part(f):
        gather(first_x + f, strips_x, im_x, every_row)
        gather_edge(strips_x, ime_x, False)
        input_ring(f)
        ux[...] = dot(x_taps(f, None, whole_tile), kernels(wg, 0, 0)) + bias(0)
        cx[...] = dot(x_taps(f, None, whole_tile), kernels(wc, 0, 0)) + bias(2)

    def state_ring(f):
        rh[...] = dot(h_taps(f, ime_h, whole_ring), kernels(wg, ch, ch))

    def state_part(f):
        gather(f, strips_h, im_h, every_row)
        gather_edge(strips_h, ime_h, True)
        state_ring(f)
        uh[...] = dot(h_taps(f, None, whole_tile), kernels(wg, ch, 0))

    def first_part():
        wait_plane(0, True)
        fill_plane(strips_h, 0)
        gather(0, strips_h, im_h, middle_rows)
        wait_plane(1, False)
        fill_plane(strips_x, 1)
        gather(first_x, strips_x, im_x, middle_rows)
        copy_wg.wait()
        copy_wc.wait()
        uh[...] = jnp.zeros_like(uh)

        def tile_part(blocks, store):
            x, h = x_taps(0, None, blocks), h_taps(0, None, blocks)
            store(ux, dot(x + h, kernels(wg, 0, 0) + kernels(wg, ch, 0)) + bias(0))
            store(cx, dot(x, kernels(wc, 0, 0)) + bias(2))

        def store_inside(ref, v):
            ref[width : tile - width, :] = v

        def store_outside(ref, v):
            ref[0:width, :] = v[0:width]
            ref[tile - width : tile, :] = v[width : 2 * width]

        tile_part(((2, height - 2),), store_inside)
        wait_vertical(0)
        fill_vertical(strips_h, 0)
        wait_vertical(1)
        fill_vertical(strips_x, 1)
        gather(0, strips_h, im_h, outer_rows)
        gather(first_x, strips_x, im_x, outer_rows)
        gather_edge(strips_h, ime_h, True)
        gather_edge(strips_x, ime_x, False)
        state_ring(0)
        input_ring(0)
        tile_part(((1, 1), (height, 1)), store_outside)

    def update_state(f):
        rs_edge[...] = sigmoid(rx[ring:, :] + rh[ring:, :]) * edge[...]
        for j in range(height + 2):
            rows = slice(j * width, (j + 1) * width)
            v = sigmoid(rx[rows, :] + rh[rows, :]) * fields[f, 1 + j].astype(f32)
            rs[j] = v.astype(bf16)
            before, after = shifted(v, rs_edge[j : j + 1, :], rs_edge[pad + j : pad + j + 1, :])
            im_rs[rows, 0:ch] = before
            im_rs[rows, ch : 2 * ch] = after
        inside = dot(
            list(taps(lambda j, rows: rs[j : j + rows], im_rs, None, ((0, height),))),
            kernels(wc, ch, 0),
        )
        for i in range(height):
            rows = slice(i * width, (i + 1) * width)
            update = sigmoid(ux[rows, :] + uh[rows, :])
            candidate = jnp.tanh(cx[rows, :] + inside[rows])
            fresh = (1.0 - update) * fields[f, 2 + i].astype(f32) + update * candidate
            fields[f + 1, 2 + i] = fresh.astype(bf16)
            stage_row(i, fresh)
        stage[f + 1] = stage32[...].astype(bf16)

    place_own().wait()
    pl.when(layer == 0)(first_part)

    def step(f, carry):
        @pl.when(jnp.logical_or(layer > 0, f > 0))
        def _():
            @pl.when(f == 0)
            def _():
                wait_plane(0, True)
                wait_vertical(0)
                fill_plane(strips_h, 0)
                fill_vertical(strips_h, 0)
                copy_wg.wait()
                copy_wc.wait()

            @pl.when(f > 0)
            def _():
                wait_halo(f)
                fill_halo(strips_h, f)

            state_part(f)

        pl.when(f > 0)(lambda: send_out(f - 1))

        @pl.when(layer > 0)
        def _():
            pass_copy(f).wait_recv()
            wait_halo(first_x + f)
            fill_halo(strips_x, first_x + f)
            input_part(f)

        update_state(f)
        pl.when(f + 1 < frame_count)(lambda: send_halo(f + 1, f + 1, 0))

        @pl.when(layer < last_layer)
        def _():
            pass_copy(f).start()
            send_halo(f + 1, first_x + f, 1)

        @pl.when(both(layer == 0, f + 1 < frame_count))
        def _():
            wait_plane(f + 2, False)
            wait_vertical(f + 2)
            fill_plane(strips_x, f + 2)
            fill_vertical(strips_x, f + 2)
            input_part(f + 1)

        return carry

    lax.fori_loop(0, frame_count, step, 0)
    send_out(frame_count - 1)

    pl.when(layer < last_layer)(lambda: sent_push(0, True))

    @pl.when(layer == last_layer)
    def _():
        for k in range(2, 1 + frame_count):
            sent_push(k, False)

    def finish(f, carry):
        pl.when(f + 1 < frame_count)(lambda: sent_halo(f + 1, 0))

        @pl.when(layer < last_layer)
        def _():
            pass_copy(f).wait_send()
            sent_halo(f + 1, 1)

        own_out(f).wait()
        drain((group - 1) * strip * width, send_sem=out_send.at[f])
        drain((group - 1) * strip * width, recv_sem=out_recv.at[f])
        return carry

    lax.fori_loop(0, frame_count, finish, 0)


def shards(count, frames, initial_state, w_gates, w_cand, biases):
    frame_count, strip, cols, ch = frames.shape
    group = 4 if count % 4 == 0 else 1
    height, width = strip * group, cols // group
    dma = pltpu.SemaphoreType.DMA
    bf16, f32 = jnp.bfloat16, jnp.float32
    anywhere = pl.BlockSpec(memory_space=pltpu.HBM)
    rows_k = w_gates.shape[2] * w_gates.shape[3]
    tile = height * width
    ring = (height + 2) * width
    pad = -(-(height + 2) // 16) * 16
    pack_rows = -(-4 * strip // 16) * 16
    held = 2 * frame_count + 1
    out = (1, frame_count, strip, cols, ch)
    return pl.pallas_call(
        functools.partial(kernel, count, group),
        out_shape=pltpu.VMEM(out, bf16),
        in_specs=[anywhere] * 4 + [pl.BlockSpec(memory_space=pltpu.VMEM)],
        out_specs=pl.BlockSpec(memory_space=pltpu.VMEM),
        scratch_shapes=[
            pltpu.VMEM((3, rows_k, 2 * ch), bf16),
            pltpu.VMEM((3, rows_k, ch), bf16),
            pltpu.VMEM((1 + frame_count, strip, cols, ch), bf16),
            pltpu.VMEM((1 + frame_count, group, pack_rows, ch), bf16),
            pltpu.VMEM((group, pack_rows, ch), f32),
            pltpu.VMEM((1 + frame_count, group + 2, pack_rows, ch), bf16),
            pltpu.VMEM((held, height + 4, width, ch), bf16),
            pltpu.VMEM((held, 6, 2 * height, ch), bf16),
            pltpu.VMEM((frame_count + 1, 2, 2 * height, ch), bf16),
            pltpu.VMEM((2, 2 * height, ch), f32),
            pltpu.VMEM((6, 3 * height, ch), f32),
            pltpu.VMEM((6, 3 * height, ch), f32),
            pltpu.VMEM(((height + 4) * width, 2 * ch), bf16),
            pltpu.VMEM((2 * pad, 9 * ch), bf16),
            pltpu.VMEM(((height + 4) * width, 2 * ch), bf16),
            pltpu.VMEM((2 * pad, 9 * ch), bf16),
            pltpu.VMEM((2 * pad, ch), f32),
            pltpu.VMEM((ring + 2 * pad, ch), f32),
            pltpu.VMEM((tile, ch), f32),
            pltpu.VMEM((tile, ch), f32),
            pltpu.VMEM((ring + 2 * pad, ch), f32),
            pltpu.VMEM((tile, ch), f32),
            pltpu.VMEM((height + 2, width, ch), bf16),
            pltpu.VMEM((ring, 2 * ch), bf16),
            pltpu.VMEM((2 * pad, ch), f32),
            pltpu.VMEM((group * (strip * width + pack_rows), ch), bf16),
            dma((2,)), dma((2 + frame_count,)),
            dma((2, 1 + frame_count)), dma((2, 1 + frame_count)),
            dma((frame_count,)), dma((frame_count,)),
            dma((frame_count,)), dma((frame_count,)), dma((frame_count,)),
            dma((2, frame_count + 1)), dma((held,)),
        ],
        compiler_params=pltpu.CompilerParams(
            collective_id=0, has_side_effects=True, vmem_limit_bytes=60_000_000
        ),
    )(
        frames,
        initial_state[0],
        w_gates.reshape(3, rows_k, 2 * ch),
        w_cand.reshape(3, rows_k, ch),
        biases,
    )


def solution(mesh):
    placed = (
        P(None, "rows", None, None),
        P("layer", "rows", None, None),
        P("layer", None, None, None, None),
        P("layer", None, None, None, None),
        P("layer", None),
    )
    return jax.shard_map(
        functools.partial(shards, mesh.shape["rows"]),
        mesh=mesh,
        in_specs=placed,
        out_specs=P("layer", None, "rows", None, None),
        check_vma=False,
    )
```

```python
import functools

import jax
import jax.numpy as jnp
from jax import lax
from jax.experimental import pallas as pl
from jax.experimental.pallas import tpu as pltpu
from jax.sharding import PartitionSpec as P

MESH = pl.DeviceIdType.MESH

ROW_DIRS = ((-1, 0), (1, 0))
COL_DIRS = ((0, -1), (0, 1), (-1, -1), (-1, 1), (1, -1), (1, 1))
DIRS = ROW_DIRS + COL_DIRS


def reorder(c, group):
    if group == 4:
        return c + (c // 2) * (5 - 2 * c)
    return c


def sigmoid(v):
    return 0.5 * jnp.tanh(0.5 * v) + 0.5


def kernel(
    count, group, frames_ref, init_ref, wg_ref, wc_ref, bias_ref, out_ref,
    wg, wc, own, packs, packs32, packed, fields, cols, stage, stage32,
    strips_x, strips_h, im_x, ime_x, im_h, ime_h, edge,
    rx, ux, cx, rh, uh, rs, im_rs, rs_edge, span,
    w_sem, load_sem, push_send, push_recv, pass_send, pass_recv,
    out_own, out_send, out_recv, halo_send, halo_recv,
):
    frame_count, strip, all_cols, ch = frames_ref.shape
    height = strip * group
    width = all_cols // group
    tile = height * width
    ring = (height + 2) * width
    pad = ime_x.shape[0] // 2
    layer = lax.axis_index("layer")
    last_layer = lax.axis_size("layer") - 1
    index = lax.axis_index("rows")
    planes = count // group
    q = index // group
    c = index % group
    t = reorder(c, group)
    first_x = frame_count + 1
    f32, bf16 = jnp.float32, jnp.bfloat16
    both = jnp.logical_and
    one = lambda cond: jnp.where(cond, 1, 0)

    def exists(step_row, step_col):
        terms = []
        if step_row < 0:
            terms.append(q > 0)
        if step_row > 0:
            terms.append(q < planes - 1)
        if step_col < 0:
            terms.append(t > 0)
        if step_col > 0:
            terms.append(t < group - 1)
        return functools.reduce(jnp.logical_and, terms)

    def at(step_row, step_col, hop=0):
        rows = (q + step_row) * group + reorder(t + step_col, group)
        return {"layer": layer + hop, "rows": rows}

    def member(d):
        return lax.rem(c + d, group)

    def send(src, dst, send_sem, recv_sem, where):
        return pltpu.make_async_remote_copy(
            src_ref=src, dst_ref=dst, send_sem=send_sem, recv_sem=recv_sem,
            device_id=where, device_id_type=MESH,
        )

    def drain(pixels, send_sem=None, recv_sem=None):
        part = span.at[pl.ds(0, pixels)]
        sem = recv_sem if send_sem is None else send_sem
        copy = send(part, part, sem, sem, {"layer": last_layer - layer})
        copy.wait_recv() if send_sem is None else copy.wait_send()

    copy_wg = pltpu.make_async_copy(wg_ref, wg, w_sem.at[0])
    copy_wc = pltpu.make_async_copy(wc_ref, wc, w_sem.at[1])
    own_cols = pl.ds(pl.multiple_of(t * width, width), width)
    own_rows = pl.ds(2 + c * strip, strip)
    inner = pl.ds(2, height)
    above, below = pl.ds(0, 2), pl.ds(height + 2, 2)

    def load(k):
        src = init_ref if k == 0 else frames_ref.at[k - 1]
        return pltpu.make_async_copy(src, own.at[k], load_sem.at[k])

    def place_own():
        return pltpu.make_async_copy(
            own.at[0, :, own_cols, :], fields.at[0, own_rows], load_sem.at[1 + frame_count]
        )

    def push(k, to_layer, skip_self):
        g = 0 if k == 0 else first_x + k - 1
        for d in range(1 if skip_self else 0, group):
            target = member(d)
            place = reorder(target, group)
            tcols = pl.ds(pl.multiple_of(place * width, width), width)
            where = {"layer": to_layer, "rows": q * group + target}
            sems = push_send.at[0, k], push_recv.at[0, k]
            send(own.at[k, :, tcols, :], fields.at[g, own_rows], *sems, where).start()
            send(packs.at[k, place], packed.at[k, c], *sems, where).start()
        for step, edge_strip, src, dst, slot in (
            (-1, 0, pl.ds(0, 2), below, group + 1), (1, group - 1, pl.ds(strip - 2, 2), above, group)
        ):
            @pl.when(both(c == edge_strip, exists(step, 0)))
            def _(step=step, src=src, dst=dst, slot=slot):
                sems = push_send.at[1, k], push_recv.at[1, k]
                for place in range(group):
                    tcols = pl.ds(place * width, width)
                    where = {"layer": to_layer, "rows": (q + step) * group + reorder(place, group)}
                    send(own.at[k, src, tcols, :], fields.at[g, dst], *sems, where).start()
                    send(packs.at[k, place], packed.at[k, slot], *sems, where).start()

    pack_rows = packs.shape[2]
    pushed = strip * width + pack_rows

    def sent_push(k, skip_self):
        drain((group - 1 if skip_self else group) * pushed, send_sem=push_send.at[0, k])
        for step, edge_strip in ((-1, 0), (1, group - 1)):
            @pl.when(both(c == edge_strip, exists(step, 0)))
            def _():
                drain(group * pushed, send_sem=push_send.at[1, k])

    def wait_plane(k, skip_self):
        drain((group - 1 if skip_self else group) * pushed, recv_sem=push_recv.at[0, k])

    def wait_vertical(k):
        for n in (1, 2):
            @pl.when(one(q > 0) + one(q < planes - 1) == n)
            def _(n=n):
                drain(n * pushed, recv_sem=push_recv.at[1, k])

    def pass_copy(f):
        return send(
            fields.at[f + 1, inner], fields.at[first_x + f, inner],
            pass_send.at[f], pass_recv.at[f], {"layer": jnp.minimum(layer + 1, last_layer)},
        )

    def own_out(f):
        return pltpu.make_async_copy(
            fields.at[f + 1, own_rows], out_ref.at[0, f, :, own_cols, :], out_own.at[f]
        )

    def send_out(f):
        for d in range(group - 1, 0, -1):
            target = member(d)
            send(
                fields.at[f + 1, pl.ds(2 + target * strip, strip)],
                out_ref.at[0, f, :, own_cols, :],
                out_send.at[f], out_recv.at[f], {"rows": q * group + target},
            ).start()
        own_out(f).start()

    def halo_copy(src, dst, k, hop):
        dr, dc = DIRS[k]
        back = DIRS.index((-dr, -dc))
        if dc == 0:
            src_ref = fields.at[src, pl.ds(2, 2) if dr < 0 else pl.ds(height, 2)]
            dst_ref = fields.at[dst, below if dr < 0 else above]
        else:
            src_ref = stage.at[src, 0 if dc < 0 else 1]
            dst_ref = cols.at[dst, back - 2]
        kind = 0 if dr == 0 else 1
        return send(
            src_ref, dst_ref, halo_send.at[hop, src], halo_recv.at[kind, dst], at(dr, dc, hop)
        )

    def send_halo(src, dst, hop):
        for k in (2, 3, 4, 5, 6, 7, 0, 1):
            pl.when(exists(*DIRS[k]))(lambda k=k: halo_copy(src, dst, k, hop).start())

    upright = one(q > 0) + one(q < planes - 1)
    sideways = one(t > 0) + one(t < group - 1)
    uprights = (1, 2) if planes > 1 else (0,)
    side_pixels, row_pixels = 2 * height, 2 * width

    def sent_halo(src, hop):
        for u in uprights:
            for v in (1, 2):
                @pl.when(both(upright == u, sideways == v))
                def _(u=u, v=v):
                    pixels = u * row_pixels + v * (1 + u) * side_pixels
                    drain(pixels, send_sem=halo_send.at[hop, src])

    def wait_sides(dst):
        for v in (1, 2):
            @pl.when(sideways == v)
            def _(v=v):
                drain(v * side_pixels, recv_sem=halo_recv.at[0, dst])

    def wait_rows(dst):
        for u in uprights:
            for v in (1, 2):
                if u:
                    @pl.when(both(upright == u, sideways == v))
                    def _(u=u, v=v):
                        drain(u * (row_pixels + v * side_pixels), recv_sem=halo_recv.at[1, dst])

    load(0).start()

    @pl.when(layer == last_layer)
    def _():
        for k in range(1, 1 + frame_count):
            load(k).start()

    copy_wg.start()
    copy_wc.start()

    barrier = pltpu.get_barrier_semaphore()
    expected = (group - 1) + group * last_layer
    for hop in range(2):
        where_layer = layer if hop == 0 else last_layer - layer
        for d in range(0 if hop else 1, group):
            pl.semaphore_signal(
                barrier, inc=1, device_id={"layer": where_layer, "rows": q * group + member(d)},
                device_id_type=MESH,
            )
        for step in (-1, 1):
            @pl.when(exists(step, 0))
            def _(step=step, where_layer=where_layer):
                for place in range(group):
                    pl.semaphore_signal(
                        barrier, inc=1,
                        device_id={"layer": where_layer, "rows": (q + step) * group + place},
                        device_id_type=MESH,
                    )

            expected = expected + group * one(exists(step, 0))

    for dr, dc in ROW_DIRS:
        @pl.when(jnp.logical_not(exists(dr, dc)))
        def _(dr=dr):
            def clear(g, carry):
                fields[g, above if dr < 0 else below] = jnp.zeros((2, width, ch), bf16)
                return carry

            lax.fori_loop(0, 2 * frame_count + 1, clear, 0)
            for k in range(1 + frame_count):
                packed[k, group if dr < 0 else group + 1] = jnp.zeros((pack_rows, ch), bf16)

    for k, (dr, dc) in enumerate(COL_DIRS):
        @pl.when(jnp.logical_not(exists(dr, dc)))
        def _(k=k):
            def clear(g, carry):
                cols[g, k] = jnp.zeros((2 * height, ch), bf16)
                return carry

            lax.fori_loop(1, 2 * frame_count + 1, clear, 0)

    strips_x[...] = jnp.zeros_like(strips_x)
    strips_h[...] = jnp.zeros_like(strips_h)
    packs32[...] = jnp.zeros_like(packs32)

    def make_packs(k):
        for place in range(group):
            for r in range(strip):
                lo, hi = place * width, (place + 1) * width
                if place > 0:
                    v = own[k, r, lo - 16 : lo, :].astype(f32)
                    packs32[place, r : r + 1, :] = v[14:15]
                    packs32[place, strip + r : strip + r + 1, :] = v[15:16]
                if place < group - 1:
                    v = own[k, r, hi : hi + 16, :].astype(f32)
                    packs32[place, 2 * strip + r : 2 * strip + r + 1, :] = v[0:1]
                    packs32[place, 3 * strip + r : 3 * strip + r + 1, :] = v[1:2]
        packs[k] = packs32[...].astype(bf16)

    load(0).wait()
    make_packs(0)
    packed[0, c] = packs[0, t]

    @pl.when(layer == last_layer)
    def _():
        for k in range(1, 1 + frame_count):
            load(k).wait()
            make_packs(k)

    pl.semaphore_wait(barrier, expected)
    place_own().start()

    @pl.when(layer < last_layer)
    def _():
        push(0, layer, True)

    @pl.when(layer == last_layer)
    def _():
        push(1, 0, False)
        sent_push(1, False)
        push(0, layer, True)
        sent_push(0, True)
        for k in range(2, 1 + frame_count):
            push(k, 0, False)

    first_col = lax.broadcasted_iota(jnp.int32, (width, ch), 0) == 0
    last_col = lax.broadcasted_iota(jnp.int32, (width, ch), 0) == width - 1

    def stage_row(i, v):
        for s, lo in enumerate((0, width - 2)):
            for k in range(2):
                stage32[s, k * height + i : k * height + i + 1, :] = v[lo + k : lo + k + 1]

    def shifted(v, left, right):
        before = jnp.where(first_col, jnp.broadcast_to(left, v.shape), pltpu.roll(v, 1, 0))
        after = jnp.where(
            last_col, jnp.broadcast_to(right, v.shape), pltpu.roll(v, width - 1, 0)
        )
        return before.astype(bf16), after.astype(bf16)

    sides = (0, 1, 4, 5)

    def fill(strips, k, slot, row):
        v = packed[k, slot].astype(f32)
        for j, s in enumerate(sides):
            strips[s, row : row + strip, :] = v[j * strip : (j + 1) * strip]

    def fill_plane(strips, k):
        for m in range(group):
            fill(strips, k, m, height + m * strip)

    def fill_vertical(strips, k):
        fill(strips, k, group, height - strip)
        fill(strips, k, group + 1, 2 * height)

    def fill_halo(strips, g, parts):
        for s in range(2):
            for part in parts:
                k = (2 + s, s, 4 + s)[part]
                v = cols[g, k].astype(f32)
                for j in range(2):
                    strips[4 * s + j, part * height : (part + 1) * height, :] = (
                        v[j * height : (j + 1) * height]
                    )

    def gather(g, strips, im, rows):
        for j in rows:
            v = fields[g, j].astype(f32)
            r = height + j - 2
            strips[2, r : r + 1, :] = v[0:1]
            strips[3, r : r + 1, :] = v[width - 1 : width]
            before, after = shifted(v, strips[1, r : r + 1, :], strips[4, r : r + 1, :])
            im[j * width : (j + 1) * width, 0:ch] = before
            im[j * width : (j + 1) * width, ch : 2 * ch] = after

    every_row = range(height + 4)
    middle_rows = range(2, height + 2)
    outer_rows = (0, 1, height + 2, height + 3)

    def gather_edge(strips, ime, keep):
        for a in range(3):
            for b in range(3):
                lo = height - 2 + a
                lanes = slice((a * 3 + b) * ch, (a * 3 + b + 1) * ch)
                ime[0:pad, lanes] = strips[b, lo : lo + pad, :].astype(bf16)
                ime[pad : 2 * pad, lanes] = strips[3 + b, lo : lo + pad, :].astype(bf16)
        if keep:
            edge[0:pad, :] = strips[1, height - 1 : height - 1 + pad, :]
            edge[pad : 2 * pad, :] = strips[4, height - 1 : height - 1 + pad, :]

    def taps(center, im, ime, blocks):
        for a in range(3):
            for b in range(3):
                pieces = []
                for row, rows in blocks:
                    j = row + a
                    if b == 1:
                        pieces.append(center(j, rows).reshape(rows * width, ch))
                    else:
                        lo = (b // 2) * ch
                        pieces.append(im[j * width : (j + rows) * width, lo : lo + ch])
                if ime is not None:
                    pieces.append(ime[:, (a * 3 + b) * ch : (a * 3 + b + 1) * ch])
                yield jnp.concatenate(pieces, axis=0) if len(pieces) > 1 else pieces[0]

    def kernels(weight, base, lo):
        return [
            weight[a, b * 2 * ch + base : b * 2 * ch + base + ch, lo : lo + ch]
            for a in range(3) for b in range(3)
        ]

    def dot(left, right):
        return jnp.dot(
            jnp.concatenate(left, axis=1), jnp.concatenate(right, axis=0),
            preferred_element_type=f32,
        )

    def x_taps(f, ime, blocks):
        g = first_x + f
        return list(taps(lambda j, rows: fields[g, j : j + rows], im_x, ime, blocks))

    def h_taps(f, ime, blocks):
        return list(taps(lambda j, rows: fields[f, j : j + rows], im_h, ime, blocks))

    whole_ring = ((0, height + 2),)
    whole_tile = ((1, height),)
    inside = ((2, height - 2),)
    ring_rest = ((0, 2), (height, 2))
    tile_rest = ((1, 1), (height, 1))
    bias = lambda n: bias_ref[:, n * ch : (n + 1) * ch]
    last = tile - width

    def store_inside(tile_ref, ring_ref, v, u):
        tile_ref[width:last, :] = v
        if ring_ref is not None:
            ring_ref[2 * width : ring - 2 * width, :] = u

    def store_tile_rest(ref, v):
        ref[0:width, :] = v[0:width]
        ref[last:tile, :] = v[width : 2 * width]

    def store_ring_rest(ref, v):
        ref[0 : 2 * width, :] = v[0 : 2 * width]
        ref[ring - 2 * width : ring + 2 * pad, :] = v[2 * width :]

    def beside(one_side, other_side):
        return [jnp.concatenate(pair, axis=1) for pair in zip(one_side, other_side)]

    def gates(base):
        return [
            wg[a, b * 2 * ch + base : b * 2 * ch + base + ch, :]
            for a in range(3) for b in range(3)
        ]

    def input_part(f):
        gather(first_x + f, strips_x, im_x, every_row)
        gather_edge(strips_x, ime_x, False)
        rx[...] = dot(x_taps(f, ime_x, whole_ring), kernels(wg, 0, ch)) + bias(1)
        v = dot(x_taps(f, None, whole_tile), beside(kernels(wg, 0, 0), kernels(wc, 0, 0)))
        ux[...] = v[:, 0:ch] + bias(0)
        cx[...] = v[:, ch : 2 * ch] + bias(2)

    def first_state_part():
        gather(0, strips_h, im_h, every_row)
        gather_edge(strips_h, ime_h, True)
        rh[...] = dot(h_taps(0, ime_h, whole_ring), kernels(wg, ch, ch))
        uh[...] = dot(h_taps(0, None, whole_tile), kernels(wg, ch, 0))

    def state_part(f):
        wait_sides(f)
        fill_halo(strips_h, f, (1,))
        gather(f, strips_h, im_h, middle_rows)
        v = dot(h_taps(f, None, inside), gates(ch))
        store_inside(uh, rh, v[:, 0:ch], v[:, ch : 2 * ch])
        wait_rows(f)
        fill_halo(strips_h, f, (0, 2))
        gather(f, strips_h, im_h, outer_rows)
        gather_edge(strips_h, ime_h, True)
        store_ring_rest(rh, dot(h_taps(f, ime_h, ring_rest), kernels(wg, ch, ch)))
        store_tile_rest(uh, dot(h_taps(f, None, tile_rest), kernels(wg, ch, 0)))

    def first_part():
        wait_plane(0, True)
        fill_plane(strips_h, 0)
        gather(0, strips_h, im_h, middle_rows)
        wait_plane(1, False)
        fill_plane(strips_x, 1)
        gather(first_x, strips_x, im_x, middle_rows)
        copy_wg.wait()
        copy_wc.wait()
        uh[...] = jnp.zeros_like(uh)
        rh[...] = jnp.zeros_like(rh)
        x, h = x_taps(0, None, inside), h_taps(0, None, inside)
        v = dot(x + h, gates(0) + gates(ch))
        store_inside(ux, rx, v[:, 0:ch] + bias(0), v[:, ch : 2 * ch] + bias(1))
        store_inside(cx, None, dot(x, kernels(wc, 0, 0)) + bias(2), None)
        wait_vertical(0)
        fill_vertical(strips_h, 0)
        gather(0, strips_h, im_h, outer_rows)
        gather_edge(strips_h, ime_h, True)
        wait_vertical(1)
        fill_vertical(strips_x, 1)
        gather(first_x, strips_x, im_x, outer_rows)
        gather_edge(strips_x, ime_x, False)
        x, h = x_taps(0, ime_x, ring_rest), h_taps(0, ime_h, ring_rest)
        store_ring_rest(rx, dot(x + h, kernels(wg, 0, ch) + kernels(wg, ch, ch)) + bias(1))
        x, h = x_taps(0, None, tile_rest), h_taps(0, None, tile_rest)
        store_tile_rest(ux, dot(x + h, kernels(wg, 0, 0) + kernels(wg, ch, 0)) + bias(0))
        store_tile_rest(cx, dot(x, kernels(wc, 0, 0)) + bias(2))

    def update_state(f):
        rs_edge[...] = sigmoid(rx[ring:, :] + rh[ring:, :]) * edge[...]
        for j in range(height + 2):
            rows = slice(j * width, (j + 1) * width)
            v = sigmoid(rx[rows, :] + rh[rows, :]) * fields[f, 1 + j].astype(f32)
            rs[j] = v.astype(bf16)
            before, after = shifted(v, rs_edge[j : j + 1, :], rs_edge[pad + j : pad + j + 1, :])
            im_rs[rows, 0:ch] = before
            im_rs[rows, ch : 2 * ch] = after
        summed = dot(
            list(taps(lambda j, rows: rs[j : j + rows], im_rs, None, ((0, height),))),
            kernels(wc, ch, 0),
        )
        for i in range(height):
            rows = slice(i * width, (i + 1) * width)
            update = sigmoid(ux[rows, :] + uh[rows, :])
            candidate = jnp.tanh(cx[rows, :] + summed[rows])
            fresh = (1.0 - update) * fields[f, 2 + i].astype(f32) + update * candidate
            fields[f + 1, 2 + i] = fresh.astype(bf16)
            stage_row(i, fresh)
        stage[f + 1] = stage32[...].astype(bf16)

    place_own().wait()
    pl.when(layer == 0)(first_part)

    @pl.when(layer > 0)
    def _():
        wait_plane(0, True)
        wait_vertical(0)
        fill_plane(strips_h, 0)
        fill_vertical(strips_h, 0)
        copy_wg.wait()
        copy_wc.wait()
        first_state_part()

    def step(f, carry):
        @pl.when(layer > 0)
        def _():
            pass_copy(f).wait_recv()
            wait_sides(first_x + f)
            wait_rows(first_x + f)
            fill_halo(strips_x, first_x + f, range(3))
            input_part(f)

        @pl.when(f > 0)
        def _():
            state_part(f)
            send_out(f - 1)

        update_state(f)
        pl.when(f + 1 < frame_count)(lambda: send_halo(f + 1, f + 1, 0))

        @pl.when(layer < last_layer)
        def _():
            pass_copy(f).start()
            send_halo(f + 1, first_x + f, 1)

        @pl.when(both(layer == 0, f + 1 < frame_count))
        def _():
            wait_plane(f + 2, False)
            wait_vertical(f + 2)
            fill_plane(strips_x, f + 2)
            fill_vertical(strips_x, f + 2)
            input_part(f + 1)

        return carry

    lax.fori_loop(0, frame_count, step, 0)
    send_out(frame_count - 1)

    pl.when(layer < last_layer)(lambda: sent_push(0, True))

    @pl.when(layer == last_layer)
    def _():
        for k in range(2, 1 + frame_count):
            sent_push(k, False)

    def finish(f, carry):
        pl.when(f + 1 < frame_count)(lambda: sent_halo(f + 1, 0))

        @pl.when(layer < last_layer)
        def _():
            pass_copy(f).wait_send()
            sent_halo(f + 1, 1)

        own_out(f).wait()
        drain((group - 1) * strip * width, send_sem=out_send.at[f])
        drain((group - 1) * strip * width, recv_sem=out_recv.at[f])
        return carry

    lax.fori_loop(0, frame_count, finish, 0)


def shards(count, frames, initial_state, w_gates, w_cand, biases):
    frame_count, strip, cols, ch = frames.shape
    group = 4 if count % 4 == 0 else 1
    height, width = strip * group, cols // group
    dma = pltpu.SemaphoreType.DMA
    bf16, f32 = jnp.bfloat16, jnp.float32
    anywhere = pl.BlockSpec(memory_space=pltpu.HBM)
    rows_k = w_gates.shape[2] * w_gates.shape[3]
    tile = height * width
    ring = (height + 2) * width
    pad = -(-(height + 2) // 16) * 16
    pack_rows = -(-4 * strip // 16) * 16
    held = 2 * frame_count + 1
    out = (1, frame_count, strip, cols, ch)
    return pl.pallas_call(
        functools.partial(kernel, count, group),
        out_shape=pltpu.VMEM(out, bf16),
        in_specs=[anywhere] * 4 + [pl.BlockSpec(memory_space=pltpu.VMEM)],
        out_specs=pl.BlockSpec(memory_space=pltpu.VMEM),
        scratch_shapes=[
            pltpu.VMEM((3, rows_k, 2 * ch), bf16),
            pltpu.VMEM((3, rows_k, ch), bf16),
            pltpu.VMEM((1 + frame_count, strip, cols, ch), bf16),
            pltpu.VMEM((1 + frame_count, group, pack_rows, ch), bf16),
            pltpu.VMEM((group, pack_rows, ch), f32),
            pltpu.VMEM((1 + frame_count, group + 2, pack_rows, ch), bf16),
            pltpu.VMEM((held, height + 4, width, ch), bf16),
            pltpu.VMEM((held, 6, 2 * height, ch), bf16),
            pltpu.VMEM((frame_count + 1, 2, 2 * height, ch), bf16),
            pltpu.VMEM((2, 2 * height, ch), f32),
            pltpu.VMEM((6, 3 * height, ch), f32),
            pltpu.VMEM((6, 3 * height, ch), f32),
            pltpu.VMEM(((height + 4) * width, 2 * ch), bf16),
            pltpu.VMEM((2 * pad, 9 * ch), bf16),
            pltpu.VMEM(((height + 4) * width, 2 * ch), bf16),
            pltpu.VMEM((2 * pad, 9 * ch), bf16),
            pltpu.VMEM((2 * pad, ch), f32),
            pltpu.VMEM((ring + 2 * pad, ch), f32),
            pltpu.VMEM((tile, ch), f32),
            pltpu.VMEM((tile, ch), f32),
            pltpu.VMEM((ring + 2 * pad, ch), f32),
            pltpu.VMEM((tile, ch), f32),
            pltpu.VMEM((height + 2, width, ch), bf16),
            pltpu.VMEM((ring, 2 * ch), bf16),
            pltpu.VMEM((2 * pad, ch), f32),
            pltpu.VMEM((group * (strip * width + pack_rows), ch), bf16),
            dma((2,)), dma((2 + frame_count,)),
            dma((2, 1 + frame_count)), dma((2, 1 + frame_count)),
            dma((frame_count,)), dma((frame_count,)),
            dma((frame_count,)), dma((frame_count,)), dma((frame_count,)),
            dma((2, frame_count + 1)), dma((2, held)),
        ],
        compiler_params=pltpu.CompilerParams(
            collective_id=0, has_side_effects=True, vmem_limit_bytes=60_000_000
        ),
    )(
        frames,
        initial_state[0],
        w_gates.reshape(3, rows_k, 2 * ch),
        w_cand.reshape(3, rows_k, ch),
        biases,
    )


def solution(mesh):
    placed = (
        P(None, "rows", None, None),
        P("layer", "rows", None, None),
        P("layer", None, None, None, None),
        P("layer", None, None, None, None),
        P("layer", None),
    )
    return jax.shard_map(
        functools.partial(shards, mesh.shape["rows"]),
        mesh=mesh,
        in_specs=placed,
        out_specs=P("layer", None, "rows", None, None),
        check_vma=False,
    )
```

```python
import functools

import jax
import jax.numpy as jnp
from jax import lax
from jax.experimental import pallas as pl
from jax.experimental.pallas import tpu as pltpu
from jax.sharding import PartitionSpec as P

MESH = pl.DeviceIdType.MESH

ROW_DIRS = ((-1, 0), (1, 0))
COL_DIRS = ((0, -1), (0, 1), (-1, -1), (-1, 1), (1, -1), (1, 1))
DIRS = ROW_DIRS + COL_DIRS


def reorder(c, group):
    if group == 4:
        return c + (c // 2) * (5 - 2 * c)
    return c


def sigmoid(v):
    return 0.5 * jnp.tanh(0.5 * v) + 0.5


def kernel(
    count, group, frames_ref, init_ref, wg_ref, wc_ref, bias_ref, out_ref,
    wg, wc, own, packs, packs32, packed, fields, cols, stage, stage32,
    strips_x, strips_h, im_x, ime_x, im_h, ime_h, edge,
    rx, ux, cx, rh, uh, rs, im_rs, rs_edge, span,
    w_sem, load_sem, push_send, push_recv, pass_send, pass_recv,
    out_own, out_send, out_recv, halo_send, halo_recv,
):
    frame_count, strip, all_cols, ch = frames_ref.shape
    height = strip * group
    width = all_cols // group
    tile = height * width
    ring = (height + 2) * width
    pad = ime_x.shape[0] // 2
    layer = lax.axis_index("layer")
    last_layer = lax.axis_size("layer") - 1
    index = lax.axis_index("rows")
    planes = count // group
    q = index // group
    c = index % group
    t = reorder(c, group)
    first_x = frame_count + 1
    f32, bf16 = jnp.float32, jnp.bfloat16
    both = jnp.logical_and
    one = lambda cond: jnp.where(cond, 1, 0)

    def exists(step_row, step_col):
        terms = []
        if step_row < 0:
            terms.append(q > 0)
        if step_row > 0:
            terms.append(q < planes - 1)
        if step_col < 0:
            terms.append(t > 0)
        if step_col > 0:
            terms.append(t < group - 1)
        return functools.reduce(jnp.logical_and, terms)

    def at(step_row, step_col, hop=0):
        rows = (q + step_row) * group + reorder(t + step_col, group)
        return {"layer": layer + hop, "rows": rows}

    def member(d):
        return lax.rem(c + d, group)

    def send(src, dst, send_sem, recv_sem, where):
        return pltpu.make_async_remote_copy(
            src_ref=src, dst_ref=dst, send_sem=send_sem, recv_sem=recv_sem,
            device_id=where, device_id_type=MESH,
        )

    def drain(pixels, send_sem=None, recv_sem=None):
        part = span.at[pl.ds(0, pixels)]
        sem = recv_sem if send_sem is None else send_sem
        copy = send(part, part, sem, sem, {"layer": last_layer - layer})
        copy.wait_recv() if send_sem is None else copy.wait_send()

    copy_wg = pltpu.make_async_copy(wg_ref, wg, w_sem.at[0])
    copy_wc = pltpu.make_async_copy(wc_ref, wc, w_sem.at[1])
    own_cols = pl.ds(pl.multiple_of(t * width, width), width)
    own_rows = pl.ds(2 + c * strip, strip)
    inner = pl.ds(2, height)
    above, below = pl.ds(0, 2), pl.ds(height + 2, 2)

    def load(k):
        src = init_ref if k == 0 else frames_ref.at[k - 1]
        return pltpu.make_async_copy(src, own.at[k], load_sem.at[k])

    def place_own():
        return pltpu.make_async_copy(
            own.at[0, :, own_cols, :], fields.at[0, own_rows], load_sem.at[1 + frame_count]
        )

    def push(k, to_layer, skip_self):
        g = 0 if k == 0 else first_x + k - 1
        for d in range(1 if skip_self else 0, group):
            target = member(d)
            place = reorder(target, group)
            tcols = pl.ds(pl.multiple_of(place * width, width), width)
            where = {"layer": to_layer, "rows": q * group + target}
            sems = push_send.at[0, k], push_recv.at[0, k]
            send(own.at[k, :, tcols, :], fields.at[g, own_rows], *sems, where).start()
            send(packs.at[k, place], packed.at[k, c], *sems, where).start()

    pack_rows = packs.shape[2]
    pushed = strip * width + pack_rows

    def relay(k):
        g = 0 if isinstance(k, int) and k == 0 else first_x + k - 1
        for step, src, dst, sent, slot in (
            (-1, pl.ds(2, 2), below, 0, group + 1),
            (1, pl.ds(height, 2), above, group - 1, group),
        ):
            @pl.when(exists(step, 0))
            def _(step=step, src=src, dst=dst, sent=sent, slot=slot):
                sems = push_send.at[1, k], push_recv.at[1, k]
                where = at(step, 0)
                send(fields.at[g, src], fields.at[g, dst], *sems, where).start()
                send(packed.at[k, sent], packed.at[k, slot], *sems, where).start()

    def sent_push(k, skip_self):
        drain((group - 1 if skip_self else group) * pushed, send_sem=push_send.at[0, k])

    def sent_relay(k):
        for n in (1, 2):
            @pl.when(one(q > 0) + one(q < planes - 1) == n)
            def _(n=n):
                drain(n * pushed, send_sem=push_send.at[1, k])

    def wait_plane(k, skip_self):
        drain((group - 1 if skip_self else group) * pushed, recv_sem=push_recv.at[0, k])

    def wait_vertical(k):
        for n in (1, 2):
            @pl.when(one(q > 0) + one(q < planes - 1) == n)
            def _(n=n):
                drain(n * pushed, recv_sem=push_recv.at[1, k])

    def pass_copy(f):
        return send(
            fields.at[f + 1, inner], fields.at[first_x + f, inner],
            pass_send.at[f], pass_recv.at[f], {"layer": jnp.minimum(layer + 1, last_layer)},
        )

    def own_out(f):
        return pltpu.make_async_copy(
            fields.at[f + 1, own_rows], out_ref.at[0, f, :, own_cols, :], out_own.at[f]
        )

    def send_out(f):
        for d in range(group - 1, 0, -1):
            target = member(d)
            send(
                fields.at[f + 1, pl.ds(2 + target * strip, strip)],
                out_ref.at[0, f, :, own_cols, :],
                out_send.at[f], out_recv.at[f], {"rows": q * group + target},
            ).start()
        own_out(f).start()

    def halo_copy(src, dst, k, hop):
        dr, dc = DIRS[k]
        back = DIRS.index((-dr, -dc))
        if dc == 0:
            src_ref = fields.at[src, pl.ds(2, 2) if dr < 0 else pl.ds(height, 2)]
            dst_ref = fields.at[dst, below if dr < 0 else above]
        else:
            src_ref = stage.at[src, 0 if dc < 0 else 1]
            dst_ref = cols.at[dst, back - 2]
        kind = 0 if dr == 0 else 1
        return send(
            src_ref, dst_ref, halo_send.at[hop, src], halo_recv.at[kind, dst], at(dr, dc, hop)
        )

    def send_halo(src, dst, hop):
        for k in (2, 3, 4, 5, 6, 7, 0, 1):
            pl.when(exists(*DIRS[k]))(lambda k=k: halo_copy(src, dst, k, hop).start())

    upright = one(q > 0) + one(q < planes - 1)
    sideways = one(t > 0) + one(t < group - 1)
    uprights = (1, 2) if planes > 1 else (0,)
    side_pixels, row_pixels = 2 * height, 2 * width

    def sent_halo(src, hop):
        for u in uprights:
            for v in (1, 2):
                @pl.when(both(upright == u, sideways == v))
                def _(u=u, v=v):
                    pixels = u * row_pixels + v * (1 + u) * side_pixels
                    drain(pixels, send_sem=halo_send.at[hop, src])

    def wait_sides(dst):
        for v in (1, 2):
            @pl.when(sideways == v)
            def _(v=v):
                drain(v * side_pixels, recv_sem=halo_recv.at[0, dst])

    def wait_rows(dst):
        for u in uprights:
            for v in (1, 2):
                if u:
                    @pl.when(both(upright == u, sideways == v))
                    def _(u=u, v=v):
                        drain(u * (row_pixels + v * side_pixels), recv_sem=halo_recv.at[1, dst])

    load(0).start()

    @pl.when(layer == last_layer)
    def _():
        for k in range(1, 1 + frame_count):
            load(k).start()

    copy_wg.start()
    copy_wc.start()

    barrier = pltpu.get_barrier_semaphore()
    expected = (group - 1) + group * last_layer
    for hop in range(2):
        where_layer = layer if hop == 0 else last_layer - layer
        for d in range(0 if hop else 1, group):
            pl.semaphore_signal(
                barrier, inc=1, device_id={"layer": where_layer, "rows": q * group + member(d)},
                device_id_type=MESH,
            )
        for dr, dc in DIRS:
            if dr != 0:
                @pl.when(exists(dr, dc))
                def _(dr=dr, dc=dc, where_layer=where_layer):
                    where = {"layer": where_layer, "rows": at(dr, dc)["rows"]}
                    pl.semaphore_signal(barrier, inc=1, device_id=where, device_id_type=MESH)

                expected = expected + one(exists(dr, dc))

    for dr, dc in ROW_DIRS:
        @pl.when(jnp.logical_not(exists(dr, dc)))
        def _(dr=dr):
            def clear(g, carry):
                fields[g, above if dr < 0 else below] = jnp.zeros((2, width, ch), bf16)
                return carry

            lax.fori_loop(0, 2 * frame_count + 1, clear, 0)
            for k in range(1 + frame_count):
                packed[k, group if dr < 0 else group + 1] = jnp.zeros((pack_rows, ch), bf16)

    for k, (dr, dc) in enumerate(COL_DIRS):
        @pl.when(jnp.logical_not(exists(dr, dc)))
        def _(k=k):
            def clear(g, carry):
                cols[g, k] = jnp.zeros((2 * height, ch), bf16)
                return carry

            lax.fori_loop(1, 2 * frame_count + 1, clear, 0)

    strips_x[...] = jnp.zeros_like(strips_x)
    strips_h[...] = jnp.zeros_like(strips_h)
    packs32[...] = jnp.zeros_like(packs32)

    def make_packs(k):
        for place in range(group):
            for r in range(strip):
                lo, hi = place * width, (place + 1) * width
                if place > 0:
                    v = own[k, r, lo - 16 : lo, :].astype(f32)
                    packs32[place, r : r + 1, :] = v[14:15]
                    packs32[place, strip + r : strip + r + 1, :] = v[15:16]
                if place < group - 1:
                    v = own[k, r, hi : hi + 16, :].astype(f32)
                    packs32[place, 2 * strip + r : 2 * strip + r + 1, :] = v[0:1]
                    packs32[place, 3 * strip + r : 3 * strip + r + 1, :] = v[1:2]
        packs[k] = packs32[...].astype(bf16)

    load(0).wait()
    make_packs(0)
    packed[0, c] = packs[0, t]

    @pl.when(layer == last_layer)
    def _():
        for k in range(1, 1 + frame_count):
            load(k).wait()
            make_packs(k)

    pl.semaphore_wait(barrier, expected)
    place_own().start()

    @pl.when(layer < last_layer)
    def _():
        push(0, layer, True)

    @pl.when(layer == last_layer)
    def _():
        push(1, 0, False)
        sent_push(1, False)
        push(0, layer, True)
        sent_push(0, True)
        for k in range(2, 1 + frame_count):
            push(k, 0, False)

    first_col = lax.broadcasted_iota(jnp.int32, (width, ch), 0) == 0
    last_col = lax.broadcasted_iota(jnp.int32, (width, ch), 0) == width - 1

    def stage_row(i, v):
        for s, lo in enumerate((0, width - 2)):
            for k in range(2):
                stage32[s, k * height + i : k * height + i + 1, :] = v[lo + k : lo + k + 1]

    def shifted(v, left, right):
        before = jnp.where(first_col, jnp.broadcast_to(left, v.shape), pltpu.roll(v, 1, 0))
        after = jnp.where(
            last_col, jnp.broadcast_to(right, v.shape), pltpu.roll(v, width - 1, 0)
        )
        return before.astype(bf16), after.astype(bf16)

    sides = (0, 1, 4, 5)

    def fill(strips, k, slot, row):
        v = packed[k, slot].astype(f32)
        for j, s in enumerate(sides):
            strips[s, row : row + strip, :] = v[j * strip : (j + 1) * strip]

    def fill_plane(strips, k):
        for m in range(group):
            fill(strips, k, m, height + m * strip)

    def fill_vertical(strips, k):
        fill(strips, k, group, height - strip)
        fill(strips, k, group + 1, 2 * height)

    def fill_halo(strips, g, parts):
        for s in range(2):
            for part in parts:
                k = (2 + s, s, 4 + s)[part]
                v = cols[g, k].astype(f32)
                for j in range(2):
                    strips[4 * s + j, part * height : (part + 1) * height, :] = (
                        v[j * height : (j + 1) * height]
                    )

    def gather(g, strips, im, rows):
        for j in rows:
            v = fields[g, j].astype(f32)
            r = height + j - 2
            strips[2, r : r + 1, :] = v[0:1]
            strips[3, r : r + 1, :] = v[width - 1 : width]
            before, after = shifted(v, strips[1, r : r + 1, :], strips[4, r : r + 1, :])
            im[j * width : (j + 1) * width, 0:ch] = before
            im[j * width : (j + 1) * width, ch : 2 * ch] = after

    every_row = range(height + 4)
    middle_rows = range(2, height + 2)
    outer_rows = (0, 1, height + 2, height + 3)

    def gather_edge(strips, ime, keep):
        for a in range(3):
            for b in range(3):
                lo = height - 2 + a
                lanes = slice((a * 3 + b) * ch, (a * 3 + b + 1) * ch)
                ime[0:pad, lanes] = strips[b, lo : lo + pad, :].astype(bf16)
                ime[pad : 2 * pad, lanes] = strips[3 + b, lo : lo + pad, :].astype(bf16)
        if keep:
            edge[0:pad, :] = strips[1, height - 1 : height - 1 + pad, :]
            edge[pad : 2 * pad, :] = strips[4, height - 1 : height - 1 + pad, :]

    def taps(center, im, ime, blocks):
        for a in range(3):
            for b in range(3):
                pieces = []
                for row, rows in blocks:
                    j = row + a
                    if b == 1:
                        pieces.append(center(j, rows).reshape(rows * width, ch))
                    else:
                        lo = (b // 2) * ch
                        pieces.append(im[j * width : (j + rows) * width, lo : lo + ch])
                if ime is not None:
                    pieces.append(ime[:, (a * 3 + b) * ch : (a * 3 + b + 1) * ch])
                yield jnp.concatenate(pieces, axis=0) if len(pieces) > 1 else pieces[0]

    def kernels(weight, base, lo):
        return [
            weight[a, b * 2 * ch + base : b * 2 * ch + base + ch, lo : lo + ch]
            for a in range(3) for b in range(3)
        ]

    def dot(left, right):
        return jnp.dot(
            jnp.concatenate(left, axis=1), jnp.concatenate(right, axis=0),
            preferred_element_type=f32,
        )

    def x_taps(f, ime, blocks):
        g = first_x + f
        return list(taps(lambda j, rows: fields[g, j : j + rows], im_x, ime, blocks))

    def h_taps(f, ime, blocks):
        return list(taps(lambda j, rows: fields[f, j : j + rows], im_h, ime, blocks))

    whole_ring = ((0, height + 2),)
    whole_tile = ((1, height),)
    inside = ((2, height - 2),)
    ring_rest = ((0, 2), (height, 2))
    tile_rest = ((1, 1), (height, 1))
    bias = lambda n: bias_ref[:, n * ch : (n + 1) * ch]
    last = tile - width

    def store_inside(tile_ref, ring_ref, v, u):
        tile_ref[width:last, :] = v
        if ring_ref is not None:
            ring_ref[2 * width : ring - 2 * width, :] = u

    def store_tile_rest(ref, v):
        ref[0:width, :] = v[0:width]
        ref[last:tile, :] = v[width : 2 * width]

    def store_ring_rest(ref, v):
        ref[0 : 2 * width, :] = v[0 : 2 * width]
        ref[ring - 2 * width : ring + 2 * pad, :] = v[2 * width :]

    def beside(one_side, other_side):
        return [jnp.concatenate(pair, axis=1) for pair in zip(one_side, other_side)]

    def gates(base):
        return [
            wg[a, b * 2 * ch + base : b * 2 * ch + base + ch, :]
            for a in range(3) for b in range(3)
        ]

    def input_part(f):
        gather(first_x + f, strips_x, im_x, every_row)
        gather_edge(strips_x, ime_x, False)
        rx[...] = dot(x_taps(f, ime_x, whole_ring), kernels(wg, 0, ch)) + bias(1)
        v = dot(x_taps(f, None, whole_tile), beside(kernels(wg, 0, 0), kernels(wc, 0, 0)))
        ux[...] = v[:, 0:ch] + bias(0)
        cx[...] = v[:, ch : 2 * ch] + bias(2)

    def first_state_part():
        gather(0, strips_h, im_h, every_row)
        gather_edge(strips_h, ime_h, True)
        rh[...] = dot(h_taps(0, ime_h, whole_ring), kernels(wg, ch, ch))
        uh[...] = dot(h_taps(0, None, whole_tile), kernels(wg, ch, 0))

    def state_part(f):
        wait_sides(f)
        fill_halo(strips_h, f, (1,))
        gather(f, strips_h, im_h, middle_rows)
        v = dot(h_taps(f, None, inside), gates(ch))
        store_inside(uh, rh, v[:, 0:ch], v[:, ch : 2 * ch])
        wait_rows(f)
        fill_halo(strips_h, f, (0, 2))
        gather(f, strips_h, im_h, outer_rows)
        gather_edge(strips_h, ime_h, True)
        store_ring_rest(rh, dot(h_taps(f, ime_h, ring_rest), kernels(wg, ch, ch)))
        store_tile_rest(uh, dot(h_taps(f, None, tile_rest), kernels(wg, ch, 0)))

    def first_part():
        wait_plane(0, True)
        relay(0)
        wait_plane(1, False)
        relay(1)
        fill_plane(strips_h, 0)
        gather(0, strips_h, im_h, middle_rows)
        fill_plane(strips_x, 1)
        gather(first_x, strips_x, im_x, middle_rows)
        copy_wg.wait()
        copy_wc.wait()
        uh[...] = jnp.zeros_like(uh)
        rh[...] = jnp.zeros_like(rh)
        x, h = x_taps(0, None, inside), h_taps(0, None, inside)
        v = dot(x + h, gates(0) + gates(ch))
        store_inside(ux, rx, v[:, 0:ch] + bias(0), v[:, ch : 2 * ch] + bias(1))
        store_inside(cx, None, dot(x, kernels(wc, 0, 0)) + bias(2), None)
        if frame_count > 1:
            wait_plane(2, False)
            relay(2)
        wait_vertical(0)
        fill_vertical(strips_h, 0)
        gather(0, strips_h, im_h, outer_rows)
        gather_edge(strips_h, ime_h, True)
        wait_vertical(1)
        fill_vertical(strips_x, 1)
        gather(first_x, strips_x, im_x, outer_rows)
        gather_edge(strips_x, ime_x, False)
        x, h = x_taps(0, ime_x, ring_rest), h_taps(0, ime_h, ring_rest)
        store_ring_rest(rx, dot(x + h, kernels(wg, 0, ch) + kernels(wg, ch, ch)) + bias(1))
        x, h = x_taps(0, None, tile_rest), h_taps(0, None, tile_rest)
        store_tile_rest(ux, dot(x + h, kernels(wg, 0, 0) + kernels(wg, ch, 0)) + bias(0))
        store_tile_rest(cx, dot(x, kernels(wc, 0, 0)) + bias(2))

    def update_state(f):
        rs_edge[...] = sigmoid(rx[ring:, :] + rh[ring:, :]) * edge[...]
        for j in range(height + 2):
            rows = slice(j * width, (j + 1) * width)
            v = sigmoid(rx[rows, :] + rh[rows, :]) * fields[f, 1 + j].astype(f32)
            rs[j] = v.astype(bf16)
            before, after = shifted(v, rs_edge[j : j + 1, :], rs_edge[pad + j : pad + j + 1, :])
            im_rs[rows, 0:ch] = before
            im_rs[rows, ch : 2 * ch] = after
        summed = dot(
            list(taps(lambda j, rows: rs[j : j + rows], im_rs, None, ((0, height),))),
            kernels(wc, ch, 0),
        )
        for i in range(height):
            rows = slice(i * width, (i + 1) * width)
            update = sigmoid(ux[rows, :] + uh[rows, :])
            candidate = jnp.tanh(cx[rows, :] + summed[rows])
            fresh = (1.0 - update) * fields[f, 2 + i].astype(f32) + update * candidate
            fields[f + 1, 2 + i] = fresh.astype(bf16)
            stage_row(i, fresh)
        stage[f + 1] = stage32[...].astype(bf16)

    place_own().wait()
    pl.when(layer == 0)(first_part)

    @pl.when(layer > 0)
    def _():
        wait_plane(0, True)
        relay(0)
        wait_vertical(0)
        fill_plane(strips_h, 0)
        fill_vertical(strips_h, 0)
        copy_wg.wait()
        copy_wc.wait()
        first_state_part()

    def step(f, carry):
        @pl.when(layer > 0)
        def _():
            pass_copy(f).wait_recv()
            wait_sides(first_x + f)
            wait_rows(first_x + f)
            fill_halo(strips_x, first_x + f, range(3))
            input_part(f)

        @pl.when(f > 0)
        def _():
            state_part(f)
            send_out(f - 1)

        @pl.when(both(layer == 0, f + 2 < frame_count))
        def _():
            wait_plane(f + 3, False)
            relay(f + 3)

        update_state(f)
        pl.when(f + 1 < frame_count)(lambda: send_halo(f + 1, f + 1, 0))

        @pl.when(layer < last_layer)
        def _():
            pass_copy(f).start()
            send_halo(f + 1, first_x + f, 1)

        @pl.when(both(layer == 0, f + 1 < frame_count))
        def _():
            wait_vertical(f + 2)
            fill_plane(strips_x, f + 2)
            fill_vertical(strips_x, f + 2)
            input_part(f + 1)

        return carry

    lax.fori_loop(0, frame_count, step, 0)
    send_out(frame_count - 1)

    sent_relay(0)

    @pl.when(layer < last_layer)
    def _():
        sent_push(0, True)
        for k in range(1, 1 + frame_count):
            sent_relay(k)

    @pl.when(layer == last_layer)
    def _():
        for k in range(2, 1 + frame_count):
            sent_push(k, False)

    def finish(f, carry):
        pl.when(f + 1 < frame_count)(lambda: sent_halo(f + 1, 0))

        @pl.when(layer < last_layer)
        def _():
            pass_copy(f).wait_send()
            sent_halo(f + 1, 1)

        own_out(f).wait()
        drain((group - 1) * strip * width, send_sem=out_send.at[f])
        drain((group - 1) * strip * width, recv_sem=out_recv.at[f])
        return carry

    lax.fori_loop(0, frame_count, finish, 0)


def shards(count, frames, initial_state, w_gates, w_cand, biases):
    frame_count, strip, cols, ch = frames.shape
    group = 4 if count % 4 == 0 else 1
    height, width = strip * group, cols // group
    dma = pltpu.SemaphoreType.DMA
    bf16, f32 = jnp.bfloat16, jnp.float32
    anywhere = pl.BlockSpec(memory_space=pltpu.HBM)
    rows_k = w_gates.shape[2] * w_gates.shape[3]
    tile = height * width
    ring = (height + 2) * width
    pad = -(-(height + 2) // 16) * 16
    pack_rows = -(-4 * strip // 16) * 16
    held = 2 * frame_count + 1
    out = (1, frame_count, strip, cols, ch)
    return pl.pallas_call(
        functools.partial(kernel, count, group),
        out_shape=pltpu.VMEM(out, bf16),
        in_specs=[anywhere] * 4 + [pl.BlockSpec(memory_space=pltpu.VMEM)],
        out_specs=pl.BlockSpec(memory_space=pltpu.VMEM),
        scratch_shapes=[
            pltpu.VMEM((3, rows_k, 2 * ch), bf16),
            pltpu.VMEM((3, rows_k, ch), bf16),
            pltpu.VMEM((1 + frame_count, strip, cols, ch), bf16),
            pltpu.VMEM((1 + frame_count, group, pack_rows, ch), bf16),
            pltpu.VMEM((group, pack_rows, ch), f32),
            pltpu.VMEM((1 + frame_count, group + 2, pack_rows, ch), bf16),
            pltpu.VMEM((held, height + 4, width, ch), bf16),
            pltpu.VMEM((held, 6, 2 * height, ch), bf16),
            pltpu.VMEM((frame_count + 1, 2, 2 * height, ch), bf16),
            pltpu.VMEM((2, 2 * height, ch), f32),
            pltpu.VMEM((6, 3 * height, ch), f32),
            pltpu.VMEM((6, 3 * height, ch), f32),
            pltpu.VMEM(((height + 4) * width, 2 * ch), bf16),
            pltpu.VMEM((2 * pad, 9 * ch), bf16),
            pltpu.VMEM(((height + 4) * width, 2 * ch), bf16),
            pltpu.VMEM((2 * pad, 9 * ch), bf16),
            pltpu.VMEM((2 * pad, ch), f32),
            pltpu.VMEM((ring + 2 * pad, ch), f32),
            pltpu.VMEM((tile, ch), f32),
            pltpu.VMEM((tile, ch), f32),
            pltpu.VMEM((ring + 2 * pad, ch), f32),
            pltpu.VMEM((tile, ch), f32),
            pltpu.VMEM((height + 2, width, ch), bf16),
            pltpu.VMEM((ring, 2 * ch), bf16),
            pltpu.VMEM((2 * pad, ch), f32),
            pltpu.VMEM((group * (strip * width + pack_rows), ch), bf16),
            dma((2,)), dma((2 + frame_count,)),
            dma((2, 1 + frame_count)), dma((2, 1 + frame_count)),
            dma((frame_count,)), dma((frame_count,)),
            dma((frame_count,)), dma((frame_count,)), dma((frame_count,)),
            dma((2, frame_count + 1)), dma((2, held)),
        ],
        compiler_params=pltpu.CompilerParams(
            collective_id=0, has_side_effects=True, vmem_limit_bytes=60_000_000
        ),
    )(
        frames,
        initial_state[0],
        w_gates.reshape(3, rows_k, 2 * ch),
        w_cand.reshape(3, rows_k, ch),
        biases,
    )


def solution(mesh):
    placed = (
        P(None, "rows", None, None),
        P("layer", "rows", None, None),
        P("layer", None, None, None, None),
        P("layer", None, None, None, None),
        P("layer", None),
    )
    return jax.shard_map(
        functools.partial(shards, mesh.shape["rows"]),
        mesh=mesh,
        in_specs=placed,
        out_specs=P("layer", None, "rows", None, None),
        check_vma=False,
    )
```

```python
import functools

import jax
import jax.numpy as jnp
from jax import lax
from jax.experimental import pallas as pl
from jax.experimental.pallas import tpu as pltpu
from jax.sharding import PartitionSpec as P

MESH = pl.DeviceIdType.MESH

ROW_DIRS = ((-1, 0), (1, 0))
COL_DIRS = ((0, -1), (0, 1), (-1, -1), (-1, 1), (1, -1), (1, 1))
DIRS = ROW_DIRS + COL_DIRS


def reorder(c, group):
    if group == 4:
        return c + (c // 2) * (5 - 2 * c)
    return c


def sigmoid(v):
    return 0.5 * jnp.tanh(0.5 * v) + 0.5


def kernel(
    count, group, frames_ref, init_ref, wg_ref, wc_ref, bias_ref, out_ref,
    wg, wc, own, packs, packs32, packed, fields, cols, stage, stage32,
    strips_x, strips_h, im_x, ime_x, im_h, ime_h, edge,
    rx, ux, cx, rh, uh, rs, im_rs, rs_edge, span,
    w_sem, load_sem, push_send, push_recv, pass_send, pass_recv,
    out_own, out_send, out_recv, halo_send, halo_recv,
):
    frame_count, strip, all_cols, ch = frames_ref.shape
    height = strip * group
    width = all_cols // group
    tile = height * width
    ring = (height + 2) * width
    pad = ime_x.shape[0] // 2
    layer = lax.axis_index("layer")
    last_layer = lax.axis_size("layer") - 1
    index = lax.axis_index("rows")
    planes = count // group
    q = index // group
    c = index % group
    t = reorder(c, group)
    first_x = frame_count + 1
    f32, bf16 = jnp.float32, jnp.bfloat16
    both = jnp.logical_and
    one = lambda cond: jnp.where(cond, 1, 0)

    def exists(step_row, step_col):
        terms = []
        if step_row < 0:
            terms.append(q > 0)
        if step_row > 0:
            terms.append(q < planes - 1)
        if step_col < 0:
            terms.append(t > 0)
        if step_col > 0:
            terms.append(t < group - 1)
        return functools.reduce(jnp.logical_and, terms)

    def at(step_row, step_col, hop=0):
        rows = (q + step_row) * group + reorder(t + step_col, group)
        return {"layer": layer + hop, "rows": rows}

    def member(d):
        return lax.rem(c + d, group)

    def others():
        if group == 4:
            return [3 - c, c + 2 - 4 * (c // 2), c + 1 - 2 * (c % 2)]
        return [member(d) for d in range(1, group)]

    def send(src, dst, send_sem, recv_sem, where):
        return pltpu.make_async_remote_copy(
            src_ref=src, dst_ref=dst, send_sem=send_sem, recv_sem=recv_sem,
            device_id=where, device_id_type=MESH,
        )

    def drain(pixels, send_sem=None, recv_sem=None):
        part = span.at[pl.ds(0, pixels)]
        sem = recv_sem if send_sem is None else send_sem
        copy = send(part, part, sem, sem, {"layer": last_layer - layer})
        copy.wait_recv() if send_sem is None else copy.wait_send()

    copy_wg = pltpu.make_async_copy(wg_ref, wg, w_sem.at[0])
    copy_wc = pltpu.make_async_copy(wc_ref, wc, w_sem.at[1])
    own_cols = pl.ds(pl.multiple_of(t * width, width), width)
    own_rows = pl.ds(2 + c * strip, strip)
    inner = pl.ds(2, height)
    above, below = pl.ds(0, 2), pl.ds(height + 2, 2)

    def load(k):
        src = init_ref if k == 0 else frames_ref.at[k - 1]
        return pltpu.make_async_copy(src, own.at[k], load_sem.at[k])

    def place_own():
        return pltpu.make_async_copy(
            own.at[0, :, own_cols, :], fields.at[0, own_rows], load_sem.at[1 + frame_count]
        )

    def push(k, to_layer, skip_self):
        g = 0 if k == 0 else first_x + k - 1
        for target in others() if skip_self else others() + [c]:
            place = reorder(target, group)
            tcols = pl.ds(pl.multiple_of(place * width, width), width)
            where = {"layer": to_layer, "rows": q * group + target}
            sems = push_send.at[0, k], push_recv.at[0, k]
            send(own.at[k, :, tcols, :], fields.at[g, own_rows], *sems, where).start()
            send(packs.at[k, place], packed.at[k, c], *sems, where).start()

    pack_rows = packs.shape[2]
    pushed = strip * width + pack_rows

    def relay(k):
        g = 0 if isinstance(k, int) and k == 0 else first_x + k - 1
        for step, src, dst, sent, slot in (
            (-1, pl.ds(2, 2), below, 0, group + 1),
            (1, pl.ds(height, 2), above, group - 1, group),
        ):
            @pl.when(exists(step, 0))
            def _(step=step, src=src, dst=dst, sent=sent, slot=slot):
                sems = push_send.at[1, k], push_recv.at[1, k]
                where = at(step, 0)
                send(fields.at[g, src], fields.at[g, dst], *sems, where).start()
                send(packed.at[k, sent], packed.at[k, slot], *sems, where).start()

    def sent_push(k, skip_self):
        drain((group - 1 if skip_self else group) * pushed, send_sem=push_send.at[0, k])

    def sent_relay(k):
        for n in (1, 2):
            @pl.when(one(q > 0) + one(q < planes - 1) == n)
            def _(n=n):
                drain(n * pushed, send_sem=push_send.at[1, k])

    def wait_plane(k, skip_self):
        drain((group - 1 if skip_self else group) * pushed, recv_sem=push_recv.at[0, k])

    def wait_vertical(k):
        for n in (1, 2):
            @pl.when(one(q > 0) + one(q < planes - 1) == n)
            def _(n=n):
                drain(n * pushed, recv_sem=push_recv.at[1, k])

    def pass_copy(f):
        return send(
            fields.at[f + 1, inner], fields.at[first_x + f, inner],
            pass_send.at[f], pass_recv.at[f], {"layer": jnp.minimum(layer + 1, last_layer)},
        )

    def own_out(f):
        return pltpu.make_async_copy(
            fields.at[f + 1, own_rows], out_ref.at[0, f, :, own_cols, :], out_own.at[f]
        )

    def send_out(f):
        for target in others():
            send(
                fields.at[f + 1, pl.ds(2 + target * strip, strip)],
                out_ref.at[0, f, :, own_cols, :],
                out_send.at[f], out_recv.at[f], {"rows": q * group + target},
            ).start()
        own_out(f).start()

    def halo_copy(src, dst, k, hop):
        dr, dc = DIRS[k]
        back = DIRS.index((-dr, -dc))
        if dc == 0:
            src_ref = fields.at[src, pl.ds(2, 2) if dr < 0 else pl.ds(height, 2)]
            dst_ref = fields.at[dst, below if dr < 0 else above]
        else:
            src_ref = stage.at[src, 0 if dc < 0 else 1]
            dst_ref = cols.at[dst, back - 2]
        kind = 0 if dr == 0 else 1
        return send(
            src_ref, dst_ref, halo_send.at[hop, src], halo_recv.at[kind, dst], at(dr, dc, hop)
        )

    side_dirs, other_dirs = (2, 3), (4, 5, 6, 7, 0, 1)

    def send_halo(src, dst, hop, dirs):
        for k in dirs:
            pl.when(exists(*DIRS[k]))(lambda k=k: halo_copy(src, dst, k, hop).start())

    upright = one(q > 0) + one(q < planes - 1)
    sideways = one(t > 0) + one(t < group - 1)
    uprights = (1, 2) if planes > 1 else (0,)
    side_pixels, row_pixels = 2 * height, 2 * width

    def sent_halo(src, hop):
        for u in uprights:
            for v in (1, 2):
                @pl.when(both(upright == u, sideways == v))
                def _(u=u, v=v):
                    pixels = u * row_pixels + v * (1 + u) * side_pixels
                    drain(pixels, send_sem=halo_send.at[hop, src])

    def wait_sides(dst):
        for v in (1, 2):
            @pl.when(sideways == v)
            def _(v=v):
                drain(v * side_pixels, recv_sem=halo_recv.at[0, dst])

    def wait_rows(dst):
        for u in uprights:
            for v in (1, 2):
                if u:
                    @pl.when(both(upright == u, sideways == v))
                    def _(u=u, v=v):
                        drain(u * (row_pixels + v * side_pixels), recv_sem=halo_recv.at[1, dst])

    load(0).start()

    @pl.when(layer == last_layer)
    def _():
        for k in range(1, 1 + frame_count):
            load(k).start()

    copy_wg.start()
    copy_wc.start()

    barrier = pltpu.get_barrier_semaphore()
    expected = (group - 1) + group * last_layer
    for hop in range(2):
        where_layer = layer if hop == 0 else last_layer - layer
        for d in range(0 if hop else 1, group):
            pl.semaphore_signal(
                barrier, inc=1, device_id={"layer": where_layer, "rows": q * group + member(d)},
                device_id_type=MESH,
            )
        for dr, dc in DIRS:
            if dr != 0:
                @pl.when(exists(dr, dc))
                def _(dr=dr, dc=dc, where_layer=where_layer):
                    where = {"layer": where_layer, "rows": at(dr, dc)["rows"]}
                    pl.semaphore_signal(barrier, inc=1, device_id=where, device_id_type=MESH)

                expected = expected + one(exists(dr, dc))

    for dr, dc in ROW_DIRS:
        @pl.when(jnp.logical_not(exists(dr, dc)))
        def _(dr=dr):
            def clear(g, carry):
                fields[g, above if dr < 0 else below] = jnp.zeros((2, width, ch), bf16)
                return carry

            lax.fori_loop(0, 2 * frame_count + 1, clear, 0)
            for k in range(1 + frame_count):
                packed[k, group if dr < 0 else group + 1] = jnp.zeros((pack_rows, ch), bf16)

    for k, (dr, dc) in enumerate(COL_DIRS):
        @pl.when(jnp.logical_not(exists(dr, dc)))
        def _(k=k):
            def clear(g, carry):
                cols[g, k] = jnp.zeros((2 * height, ch), bf16)
                return carry

            lax.fori_loop(1, 2 * frame_count + 1, clear, 0)

    strips_x[...] = jnp.zeros_like(strips_x)
    strips_h[...] = jnp.zeros_like(strips_h)
    packs32[...] = jnp.zeros_like(packs32)

    def make_packs(k):
        for place in range(group):
            for r in range(strip):
                lo, hi = place * width, (place + 1) * width
                if place > 0:
                    v = own[k, r, lo - 16 : lo, :].astype(f32)
                    packs32[place, r : r + 1, :] = v[14:15]
                    packs32[place, strip + r : strip + r + 1, :] = v[15:16]
                if place < group - 1:
                    v = own[k, r, hi : hi + 16, :].astype(f32)
                    packs32[place, 2 * strip + r : 2 * strip + r + 1, :] = v[0:1]
                    packs32[place, 3 * strip + r : 3 * strip + r + 1, :] = v[1:2]
        packs[k] = packs32[...].astype(bf16)

    load(0).wait()
    make_packs(0)
    packed[0, c] = packs[0, t]

    @pl.when(layer == last_layer)
    def _():
        for k in range(1, 1 + frame_count):
            load(k).wait()
            make_packs(k)

    pl.semaphore_wait(barrier, expected)
    place_own().start()

    @pl.when(layer < last_layer)
    def _():
        push(0, layer, True)

    @pl.when(layer == last_layer)
    def _():
        push(1, 0, False)
        sent_push(1, False)
        push(0, layer, True)
        sent_push(0, True)
        for k in range(2, 1 + frame_count):
            push(k, 0, False)

    first_col = lax.broadcasted_iota(jnp.int32, (width, ch), 0) == 0
    last_col = lax.broadcasted_iota(jnp.int32, (width, ch), 0) == width - 1

    def stage_row(i, v):
        for s, lo in enumerate((0, width - 2)):
            for k in range(2):
                stage32[s, k * height + i : k * height + i + 1, :] = v[lo + k : lo + k + 1]

    def shifted(v, left, right):
        before = jnp.where(first_col, jnp.broadcast_to(left, v.shape), pltpu.roll(v, 1, 0))
        after = jnp.where(
            last_col, jnp.broadcast_to(right, v.shape), pltpu.roll(v, width - 1, 0)
        )
        return before.astype(bf16), after.astype(bf16)

    sides = (0, 1, 4, 5)

    def fill(strips, k, slot, row):
        v = packed[k, slot].astype(f32)
        for j, s in enumerate(sides):
            strips[s, row : row + strip, :] = v[j * strip : (j + 1) * strip]

    def fill_plane(strips, k):
        for m in range(group):
            fill(strips, k, m, height + m * strip)

    def fill_vertical(strips, k):
        fill(strips, k, group, height - strip)
        fill(strips, k, group + 1, 2 * height)

    def fill_halo(strips, g, parts):
        for s in range(2):
            for part in parts:
                k = (2 + s, s, 4 + s)[part]
                v = cols[g, k].astype(f32)
                for j in range(2):
                    strips[4 * s + j, part * height : (part + 1) * height, :] = (
                        v[j * height : (j + 1) * height]
                    )

    def gather(g, strips, im, rows):
        for j in rows:
            v = fields[g, j].astype(f32)
            r = height + j - 2
            strips[2, r : r + 1, :] = v[0:1]
            strips[3, r : r + 1, :] = v[width - 1 : width]
            before, after = shifted(v, strips[1, r : r + 1, :], strips[4, r : r + 1, :])
            im[j * width : (j + 1) * width, 0:ch] = before
            im[j * width : (j + 1) * width, ch : 2 * ch] = after

    every_row = range(height + 4)
    middle_rows = range(2, height + 2)
    outer_rows = (0, 1, height + 2, height + 3)

    def gather_edge(strips, ime, keep):
        for a in range(3):
            for b in range(3):
                lo = height - 2 + a
                lanes = slice((a * 3 + b) * ch, (a * 3 + b + 1) * ch)
                ime[0:pad, lanes] = strips[b, lo : lo + pad, :].astype(bf16)
                ime[pad : 2 * pad, lanes] = strips[3 + b, lo : lo + pad, :].astype(bf16)
        if keep:
            edge[0:pad, :] = strips[1, height - 1 : height - 1 + pad, :]
            edge[pad : 2 * pad, :] = strips[4, height - 1 : height - 1 + pad, :]

    def taps(center, im, ime, blocks):
        for a in range(3):
            for b in range(3):
                pieces = []
                for row, rows in blocks:
                    j = row + a
                    if b == 1:
                        pieces.append(center(j, rows).reshape(rows * width, ch))
                    else:
                        lo = (b // 2) * ch
                        pieces.append(im[j * width : (j + rows) * width, lo : lo + ch])
                if ime is not None:
                    pieces.append(ime[:, (a * 3 + b) * ch : (a * 3 + b + 1) * ch])
                yield jnp.concatenate(pieces, axis=0) if len(pieces) > 1 else pieces[0]

    def kernels(weight, base, lo):
        return [
            weight[a, b * 2 * ch + base : b * 2 * ch + base + ch, lo : lo + ch]
            for a in range(3) for b in range(3)
        ]

    def dot(left, right):
        return jnp.dot(
            jnp.concatenate(left, axis=1), jnp.concatenate(right, axis=0),
            preferred_element_type=f32,
        )

    def x_taps(f, ime, blocks):
        g = first_x + f
        return list(taps(lambda j, rows: fields[g, j : j + rows], im_x, ime, blocks))

    def h_taps(f, ime, blocks):
        return list(taps(lambda j, rows: fields[f, j : j + rows], im_h, ime, blocks))

    whole_ring = ((0, height + 2),)
    whole_tile = ((1, height),)
    inside = ((2, height - 2),)
    ring_rest = ((0, 2), (height, 2))
    tile_rest = ((1, 1), (height, 1))
    bias = lambda n: bias_ref[:, n * ch : (n + 1) * ch]
    last = tile - width

    def store_inside(tile_ref, ring_ref, v, u):
        tile_ref[width:last, :] = v
        if ring_ref is not None:
            ring_ref[2 * width : ring - 2 * width, :] = u

    def store_tile_rest(ref, v):
        ref[0:width, :] = v[0:width]
        ref[last:tile, :] = v[width : 2 * width]

    def store_ring_rest(ref, v):
        ref[0 : 2 * width, :] = v[0 : 2 * width]
        ref[ring - 2 * width : ring + 2 * pad, :] = v[2 * width :]

    def beside(one_side, other_side):
        return [jnp.concatenate(pair, axis=1) for pair in zip(one_side, other_side)]

    def gates(base):
        return [
            wg[a, b * 2 * ch + base : b * 2 * ch + base + ch, :]
            for a in range(3) for b in range(3)
        ]

    def input_part(f):
        gather(first_x + f, strips_x, im_x, every_row)
        gather_edge(strips_x, ime_x, False)
        rx[...] = dot(x_taps(f, ime_x, whole_ring), kernels(wg, 0, ch)) + bias(1)
        v = dot(x_taps(f, None, whole_tile), beside(kernels(wg, 0, 0), kernels(wc, 0, 0)))
        ux[...] = v[:, 0:ch] + bias(0)
        cx[...] = v[:, ch : 2 * ch] + bias(2)

    def passed_input_part(f):
        g = first_x + f
        pass_copy(f).wait_recv()
        wait_sides(g)
        fill_halo(strips_x, g, (1,))
        gather(g, strips_x, im_x, middle_rows)
        v = dot(x_taps(f, None, inside), beside(gates(0), kernels(wc, 0, 0)))
        store_inside(ux, rx, v[:, 0:ch] + bias(0), v[:, ch : 2 * ch] + bias(1))
        store_inside(cx, None, v[:, 2 * ch : 3 * ch] + bias(2), None)
        wait_rows(g)
        fill_halo(strips_x, g, (0, 2))
        gather(g, strips_x, im_x, outer_rows)
        gather_edge(strips_x, ime_x, False)
        store_ring_rest(rx, dot(x_taps(f, ime_x, ring_rest), kernels(wg, 0, ch)) + bias(1))
        v = dot(x_taps(f, None, tile_rest), beside(kernels(wg, 0, 0), kernels(wc, 0, 0)))
        store_tile_rest(ux, v[:, 0:ch] + bias(0))
        store_tile_rest(cx, v[:, ch : 2 * ch] + bias(2))

    def first_state_part():
        gather(0, strips_h, im_h, every_row)
        gather_edge(strips_h, ime_h, True)
        rh[...] = dot(h_taps(0, ime_h, whole_ring), kernels(wg, ch, ch))
        uh[...] = dot(h_taps(0, None, whole_tile), kernels(wg, ch, 0))

    def state_part(f):
        wait_sides(f)
        fill_halo(strips_h, f, (1,))
        gather(f, strips_h, im_h, middle_rows)
        v = dot(h_taps(f, None, inside), gates(ch))
        store_inside(uh, rh, v[:, 0:ch], v[:, ch : 2 * ch])
        wait_rows(f)
        send_out(f - 1)
        fill_halo(strips_h, f, (0, 2))
        gather(f, strips_h, im_h, outer_rows)
        gather_edge(strips_h, ime_h, True)
        store_ring_rest(rh, dot(h_taps(f, ime_h, ring_rest), kernels(wg, ch, ch)))
        store_tile_rest(uh, dot(h_taps(f, None, tile_rest), kernels(wg, ch, 0)))

    def first_part():
        wait_plane(0, True)
        relay(0)
        wait_plane(1, False)
        relay(1)
        fill_plane(strips_h, 0)
        gather(0, strips_h, im_h, middle_rows)
        fill_plane(strips_x, 1)
        gather(first_x, strips_x, im_x, middle_rows)
        copy_wg.wait()
        copy_wc.wait()
        uh[...] = jnp.zeros_like(uh)
        rh[...] = jnp.zeros_like(rh)
        x, h = x_taps(0, None, inside), h_taps(0, None, inside)
        v = dot(x + h, gates(0) + gates(ch))
        store_inside(ux, rx, v[:, 0:ch] + bias(0), v[:, ch : 2 * ch] + bias(1))
        store_inside(cx, None, dot(x, kernels(wc, 0, 0)) + bias(2), None)
        if frame_count > 1:
            wait_plane(2, False)
            relay(2)
        wait_vertical(0)
        fill_vertical(strips_h, 0)
        gather(0, strips_h, im_h, outer_rows)
        gather_edge(strips_h, ime_h, True)
        wait_vertical(1)
        fill_vertical(strips_x, 1)
        gather(first_x, strips_x, im_x, outer_rows)
        gather_edge(strips_x, ime_x, False)
        x, h = x_taps(0, ime_x, ring_rest), h_taps(0, ime_h, ring_rest)
        store_ring_rest(rx, dot(x + h, kernels(wg, 0, ch) + kernels(wg, ch, ch)) + bias(1))
        x, h = x_taps(0, None, tile_rest), h_taps(0, None, tile_rest)
        store_tile_rest(ux, dot(x + h, kernels(wg, 0, 0) + kernels(wg, ch, 0)) + bias(0))
        store_tile_rest(cx, dot(x, kernels(wc, 0, 0)) + bias(2))

    def update_state(f):
        rs_edge[...] = sigmoid(rx[ring:, :] + rh[ring:, :]) * edge[...]
        for j in range(height + 2):
            rows = slice(j * width, (j + 1) * width)
            v = sigmoid(rx[rows, :] + rh[rows, :]) * fields[f, 1 + j].astype(f32)
            rs[j] = v.astype(bf16)
            before, after = shifted(v, rs_edge[j : j + 1, :], rs_edge[pad + j : pad + j + 1, :])
            im_rs[rows, 0:ch] = before
            im_rs[rows, ch : 2 * ch] = after
        summed = dot(
            list(taps(lambda j, rows: rs[j : j + rows], im_rs, None, ((0, height),))),
            kernels(wc, ch, 0),
        )
        for i in range(height):
            rows = slice(i * width, (i + 1) * width)
            update = sigmoid(ux[rows, :] + uh[rows, :])
            candidate = jnp.tanh(cx[rows, :] + summed[rows])
            fresh = (1.0 - update) * fields[f, 2 + i].astype(f32) + update * candidate
            fields[f + 1, 2 + i] = fresh.astype(bf16)
            stage_row(i, fresh)
        stage[f + 1] = stage32[...].astype(bf16)

    place_own().wait()
    pl.when(layer == 0)(first_part)

    @pl.when(layer > 0)
    def _():
        wait_plane(0, True)
        relay(0)
        wait_vertical(0)
        fill_plane(strips_h, 0)
        fill_vertical(strips_h, 0)
        copy_wg.wait()
        copy_wc.wait()
        first_state_part()

    def step(f, carry):
        @pl.when(layer > 0)
        def _():
            passed_input_part(f)

        @pl.when(f > 0)
        def _():
            state_part(f)

        @pl.when(both(layer == 0, f + 2 < frame_count))
        def _():
            wait_plane(f + 3, False)
            relay(f + 3)

        update_state(f)
        more, onward = f + 1 < frame_count, layer < last_layer
        pl.when(more)(lambda: send_halo(f + 1, f + 1, 0, side_dirs))
        pl.when(onward)(lambda: send_halo(f + 1, first_x + f, 1, side_dirs))
        pl.when(more)(lambda: send_halo(f + 1, f + 1, 0, other_dirs))

        @pl.when(onward)
        def _():
            pass_copy(f).start()
            send_halo(f + 1, first_x + f, 1, other_dirs)

        @pl.when(both(layer == 0, f + 1 < frame_count))
        def _():
            wait_vertical(f + 2)
            fill_plane(strips_x, f + 2)
            fill_vertical(strips_x, f + 2)
            input_part(f + 1)

        return carry

    lax.fori_loop(0, frame_count, step, 0)
    send_out(frame_count - 1)

    sent_relay(0)

    @pl.when(layer < last_layer)
    def _():
        sent_push(0, True)
        for k in range(1, 1 + frame_count):
            sent_relay(k)

    @pl.when(layer == last_layer)
    def _():
        for k in range(2, 1 + frame_count):
            sent_push(k, False)

    def finish(f, carry):
        pl.when(f + 1 < frame_count)(lambda: sent_halo(f + 1, 0))

        @pl.when(layer < last_layer)
        def _():
            pass_copy(f).wait_send()
            sent_halo(f + 1, 1)

        own_out(f).wait()
        drain((group - 1) * strip * width, send_sem=out_send.at[f])
        drain((group - 1) * strip * width, recv_sem=out_recv.at[f])
        return carry

    lax.fori_loop(0, frame_count, finish, 0)


def shards(count, frames, initial_state, w_gates, w_cand, biases):
    frame_count, strip, cols, ch = frames.shape
    group = 4 if count % 4 == 0 else 1
    height, width = strip * group, cols // group
    dma = pltpu.SemaphoreType.DMA
    bf16, f32 = jnp.bfloat16, jnp.float32
    anywhere = pl.BlockSpec(memory_space=pltpu.HBM)
    rows_k = w_gates.shape[2] * w_gates.shape[3]
    tile = height * width
    ring = (height + 2) * width
    pad = -(-(height + 2) // 16) * 16
    pack_rows = -(-4 * strip // 16) * 16
    held = 2 * frame_count + 1
    out = (1, frame_count, strip, cols, ch)
    return pl.pallas_call(
        functools.partial(kernel, count, group),
        out_shape=pltpu.VMEM(out, bf16),
        in_specs=[anywhere] * 4 + [pl.BlockSpec(memory_space=pltpu.VMEM)],
        out_specs=pl.BlockSpec(memory_space=pltpu.VMEM),
        scratch_shapes=[
            pltpu.VMEM((3, rows_k, 2 * ch), bf16),
            pltpu.VMEM((3, rows_k, ch), bf16),
            pltpu.VMEM((1 + frame_count, strip, cols, ch), bf16),
            pltpu.VMEM((1 + frame_count, group, pack_rows, ch), bf16),
            pltpu.VMEM((group, pack_rows, ch), f32),
            pltpu.VMEM((1 + frame_count, group + 2, pack_rows, ch), bf16),
            pltpu.VMEM((held, height + 4, width, ch), bf16),
            pltpu.VMEM((held, 6, 2 * height, ch), bf16),
            pltpu.VMEM((frame_count + 1, 2, 2 * height, ch), bf16),
            pltpu.VMEM((2, 2 * height, ch), f32),
            pltpu.VMEM((6, 3 * height, ch), f32),
            pltpu.VMEM((6, 3 * height, ch), f32),
            pltpu.VMEM(((height + 4) * width, 2 * ch), bf16),
            pltpu.VMEM((2 * pad, 9 * ch), bf16),
            pltpu.VMEM(((height + 4) * width, 2 * ch), bf16),
            pltpu.VMEM((2 * pad, 9 * ch), bf16),
            pltpu.VMEM((2 * pad, ch), f32),
            pltpu.VMEM((ring + 2 * pad, ch), f32),
            pltpu.VMEM((tile, ch), f32),
            pltpu.VMEM((tile, ch), f32),
            pltpu.VMEM((ring + 2 * pad, ch), f32),
            pltpu.VMEM((tile, ch), f32),
            pltpu.VMEM((height + 2, width, ch), bf16),
            pltpu.VMEM((ring, 2 * ch), bf16),
            pltpu.VMEM((2 * pad, ch), f32),
            pltpu.VMEM((group * (strip * width + pack_rows), ch), bf16),
            dma((2,)), dma((2 + frame_count,)),
            dma((2, 1 + frame_count)), dma((2, 1 + frame_count)),
            dma((frame_count,)), dma((frame_count,)),
            dma((frame_count,)), dma((frame_count,)), dma((frame_count,)),
            dma((2, frame_count + 1)), dma((2, held)),
        ],
        compiler_params=pltpu.CompilerParams(
            collective_id=0, has_side_effects=True, vmem_limit_bytes=60_000_000
        ),
    )(
        frames,
        initial_state[0],
        w_gates.reshape(3, rows_k, 2 * ch),
        w_cand.reshape(3, rows_k, ch),
        biases,
    )


def solution(mesh):
    placed = (
        P(None, "rows", None, None),
        P("layer", "rows", None, None),
        P("layer", None, None, None, None),
        P("layer", None, None, None, None),
        P("layer", None),
    )
    return jax.shard_map(
        functools.partial(shards, mesh.shape["rows"]),
        mesh=mesh,
        in_specs=placed,
        out_specs=P("layer", None, "rows", None, None),
        check_vma=False,
    )
```

```python
import functools

import jax
import jax.numpy as jnp
from jax import lax
from jax.experimental import pallas as pl
from jax.experimental.pallas import tpu as pltpu
from jax.sharding import PartitionSpec as P

MESH = pl.DeviceIdType.MESH

ROW_DIRS = ((-1, 0), (1, 0))
COL_DIRS = ((0, -1), (0, 1), (-1, -1), (-1, 1), (1, -1), (1, 1))
DIRS = ROW_DIRS + COL_DIRS


def reorder(c, group):
    if group == 4:
        return c + (c // 2) * (5 - 2 * c)
    return c


def sigmoid(v):
    return 0.5 * jnp.tanh(0.5 * v) + 0.5


def kernel(
    count, group, frames_ref, init_ref, wg_ref, wc_ref, bias_ref, out_ref,
    wg, wc, own, packs, packs32, packed, fields, cols, stage, stage32,
    strips_x, strips_h, im_x, ime_x, im_h, ime_h, edge,
    rx, ux, cx, rh, uh, rs, im_rs, rs_edge, span,
    w_sem, load_sem, push_send, push_recv, pass_send, pass_recv,
    out_own, out_send, out_recv, halo_send, halo_recv,
):
    frame_count, strip, all_cols, ch = frames_ref.shape
    height = strip * group
    width = all_cols // group
    tile = height * width
    ring = (height + 2) * width
    pad = ime_x.shape[0] // 2
    layer = lax.axis_index("layer")
    last_layer = lax.axis_size("layer") - 1
    index = lax.axis_index("rows")
    planes = count // group
    q = index // group
    c = index % group
    t = reorder(c, group)
    first_x = frame_count + 1
    f32, bf16 = jnp.float32, jnp.bfloat16
    both = jnp.logical_and
    one = lambda cond: jnp.where(cond, 1, 0)

    def exists(step_row, step_col):
        terms = []
        if step_row < 0:
            terms.append(q > 0)
        if step_row > 0:
            terms.append(q < planes - 1)
        if step_col < 0:
            terms.append(t > 0)
        if step_col > 0:
            terms.append(t < group - 1)
        return functools.reduce(jnp.logical_and, terms)

    def at(step_row, step_col, hop=0):
        rows = (q + step_row) * group + reorder(t + step_col, group)
        return {"layer": layer + hop, "rows": rows}

    def member(d):
        return lax.rem(c + d, group)

    def others():
        if group == 4:
            return [3 - c, c + 2 - 4 * (c // 2), c + 1 - 2 * (c % 2)]
        return [member(d) for d in range(1, group)]

    def send(src, dst, send_sem, recv_sem, where):
        return pltpu.make_async_remote_copy(
            src_ref=src, dst_ref=dst, send_sem=send_sem, recv_sem=recv_sem,
            device_id=where, device_id_type=MESH,
        )

    def drain(pixels, send_sem=None, recv_sem=None):
        part = span.at[pl.ds(0, pixels)]
        sem = recv_sem if send_sem is None else send_sem
        copy = send(part, part, sem, sem, {"layer": last_layer - layer})
        copy.wait_recv() if send_sem is None else copy.wait_send()

    copy_wg = pltpu.make_async_copy(wg_ref, wg, w_sem.at[0])
    copy_wc = pltpu.make_async_copy(wc_ref, wc, w_sem.at[1])
    own_cols = pl.ds(pl.multiple_of(t * width, width), width)
    own_rows = pl.ds(2 + c * strip, strip)
    inner = pl.ds(2, height)
    above, below = pl.ds(0, 2), pl.ds(height + 2, 2)

    def load(k):
        src = init_ref if k == 0 else frames_ref.at[k - 1]
        return pltpu.make_async_copy(src, own.at[k], load_sem.at[k])

    def place_own():
        return pltpu.make_async_copy(
            own.at[0, :, own_cols, :], fields.at[0, own_rows], load_sem.at[1 + frame_count]
        )

    def push(k, to_layer, skip_self):
        g = 0 if k == 0 else first_x + k - 1
        for target in others() if skip_self else others() + [c]:
            place = reorder(target, group)
            tcols = pl.ds(pl.multiple_of(place * width, width), width)
            where = {"layer": to_layer, "rows": q * group + target}
            sems = push_send.at[0, k], push_recv.at[0, k]
            send(own.at[k, :, tcols, :], fields.at[g, own_rows], *sems, where).start()
            send(packs.at[k, place], packed.at[k, c], *sems, where).start()

    pack_rows = packs.shape[2]
    pushed = strip * width + pack_rows

    def relay(k):
        g = 0 if isinstance(k, int) and k == 0 else first_x + k - 1
        for step, src, dst, sent, slot in (
            (-1, pl.ds(2, 2), below, 0, group + 1),
            (1, pl.ds(height, 2), above, group - 1, group),
        ):
            @pl.when(exists(step, 0))
            def _(step=step, src=src, dst=dst, sent=sent, slot=slot):
                sems = push_send.at[1, k], push_recv.at[1, k]
                where = at(step, 0)
                send(fields.at[g, src], fields.at[g, dst], *sems, where).start()
                send(packed.at[k, sent], packed.at[k, slot], *sems, where).start()

    def sent_push(k, skip_self):
        drain((group - 1 if skip_self else group) * pushed, send_sem=push_send.at[0, k])

    def sent_relay(k):
        for n in (1, 2):
            @pl.when(one(q > 0) + one(q < planes - 1) == n)
            def _(n=n):
                drain(n * pushed, send_sem=push_send.at[1, k])

    def wait_plane(k, skip_self):
        drain((group - 1 if skip_self else group) * pushed, recv_sem=push_recv.at[0, k])

    def wait_vertical(k):
        for n in (1, 2):
            @pl.when(one(q > 0) + one(q < planes - 1) == n)
            def _(n=n):
                drain(n * pushed, recv_sem=push_recv.at[1, k])

    def pass_copy(f):
        return send(
            fields.at[f + 1, inner], fields.at[first_x + f, inner],
            pass_send.at[f], pass_recv.at[f], {"layer": jnp.minimum(layer + 1, last_layer)},
        )

    def own_out(f):
        return pltpu.make_async_copy(
            fields.at[f + 1, own_rows], out_ref.at[0, f, :, own_cols, :], out_own.at[f]
        )

    def send_out(f):
        for target in others():
            send(
                fields.at[f + 1, pl.ds(2 + target * strip, strip)],
                out_ref.at[0, f, :, own_cols, :],
                out_send.at[f], out_recv.at[f], {"rows": q * group + target},
            ).start()
        own_out(f).start()

    def halo_copy(src, dst, k, hop):
        dr, dc = DIRS[k]
        back = DIRS.index((-dr, -dc))
        if dc == 0:
            src_ref = fields.at[src, pl.ds(2, 2) if dr < 0 else pl.ds(height, 2)]
            dst_ref = fields.at[dst, below if dr < 0 else above]
        else:
            src_ref = stage.at[src, 0 if dc < 0 else 1]
            dst_ref = cols.at[dst, back - 2]
        kind = 0 if dr == 0 else 1
        return send(
            src_ref, dst_ref, halo_send.at[hop, src], halo_recv.at[kind, dst], at(dr, dc, hop)
        )

    side_dirs, other_dirs = (2, 3), (4, 5, 6, 7, 0, 1)

    def send_halo(src, dst, hop, dirs):
        for k in dirs:
            pl.when(exists(*DIRS[k]))(lambda k=k: halo_copy(src, dst, k, hop).start())

    upright = one(q > 0) + one(q < planes - 1)
    sideways = one(t > 0) + one(t < group - 1)
    uprights = (1, 2) if planes > 1 else (0,)
    side_pixels, row_pixels = 2 * height, 2 * width

    def sent_halo(src, hop):
        for u in uprights:
            for v in (1, 2):
                @pl.when(both(upright == u, sideways == v))
                def _(u=u, v=v):
                    pixels = u * row_pixels + v * (1 + u) * side_pixels
                    drain(pixels, send_sem=halo_send.at[hop, src])

    def wait_sides(dst):
        for v in (1, 2):
            @pl.when(sideways == v)
            def _(v=v):
                drain(v * side_pixels, recv_sem=halo_recv.at[0, dst])

    def wait_rows(dst):
        for u in uprights:
            for v in (1, 2):
                if u:
                    @pl.when(both(upright == u, sideways == v))
                    def _(u=u, v=v):
                        drain(u * (row_pixels + v * side_pixels), recv_sem=halo_recv.at[1, dst])

    load(0).start()

    @pl.when(layer == last_layer)
    def _():
        for k in range(1, 1 + frame_count):
            load(k).start()

    copy_wg.start()
    copy_wc.start()

    barrier = pltpu.get_barrier_semaphore()
    expected = (group - 1) + group * last_layer
    for hop in range(2):
        where_layer = layer if hop == 0 else last_layer - layer
        for d in range(0 if hop else 1, group):
            pl.semaphore_signal(
                barrier, inc=1, device_id={"layer": where_layer, "rows": q * group + member(d)},
                device_id_type=MESH,
            )
        for dr, dc in DIRS:
            if dr != 0:
                @pl.when(exists(dr, dc))
                def _(dr=dr, dc=dc, where_layer=where_layer):
                    where = {"layer": where_layer, "rows": at(dr, dc)["rows"]}
                    pl.semaphore_signal(barrier, inc=1, device_id=where, device_id_type=MESH)

                expected = expected + one(exists(dr, dc))

    for dr, dc in ROW_DIRS:
        @pl.when(jnp.logical_not(exists(dr, dc)))
        def _(dr=dr):
            def clear(g, carry):
                fields[g, above if dr < 0 else below] = jnp.zeros((2, width, ch), bf16)
                return carry

            lax.fori_loop(0, 2 * frame_count + 1, clear, 0)
            for k in range(1 + frame_count):
                packed[k, group if dr < 0 else group + 1] = jnp.zeros((pack_rows, ch), bf16)

    for k, (dr, dc) in enumerate(COL_DIRS):
        @pl.when(jnp.logical_not(exists(dr, dc)))
        def _(k=k):
            def clear(g, carry):
                cols[g, k] = jnp.zeros((2 * height, ch), bf16)
                return carry

            lax.fori_loop(1, 2 * frame_count + 1, clear, 0)

    strips_x[...] = jnp.zeros_like(strips_x)
    strips_h[...] = jnp.zeros_like(strips_h)
    packs32[...] = jnp.zeros_like(packs32)

    def make_packs(k):
        for place in range(group):
            for r in range(strip):
                lo, hi = place * width, (place + 1) * width
                if place > 0:
                    v = own[k, r, lo - 16 : lo, :].astype(f32)
                    packs32[place, r : r + 1, :] = v[14:15]
                    packs32[place, strip + r : strip + r + 1, :] = v[15:16]
                if place < group - 1:
                    v = own[k, r, hi : hi + 16, :].astype(f32)
                    packs32[place, 2 * strip + r : 2 * strip + r + 1, :] = v[0:1]
                    packs32[place, 3 * strip + r : 3 * strip + r + 1, :] = v[1:2]
        packs[k] = packs32[...].astype(bf16)

    @pl.when(layer == last_layer)
    def _():
        load(1).wait()
        make_packs(1)

    @pl.when(layer < last_layer)
    def _():
        load(0).wait()
        make_packs(0)

    pl.semaphore_wait(barrier, expected)

    @pl.when(layer < last_layer)
    def _():
        push(0, layer, True)

    @pl.when(layer == last_layer)
    def _():
        push(1, 0, False)
        load(0).wait()
        make_packs(0)
        for k in range(2, 1 + frame_count):
            load(k).wait()
            make_packs(k)
        sent_push(1, False)
        push(0, layer, True)
        sent_push(0, True)
        for k in range(2, 1 + frame_count):
            push(k, 0, False)

    packed[0, c] = packs[0, t]
    place_own().start()

    first_col = lax.broadcasted_iota(jnp.int32, (width, ch), 0) == 0
    last_col = lax.broadcasted_iota(jnp.int32, (width, ch), 0) == width - 1

    def stage_row(i, v):
        for s, lo in enumerate((0, width - 2)):
            for k in range(2):
                stage32[s, k * height + i : k * height + i + 1, :] = v[lo + k : lo + k + 1]

    def shifted(v, left, right):
        before = jnp.where(first_col, jnp.broadcast_to(left, v.shape), pltpu.roll(v, 1, 0))
        after = jnp.where(
            last_col, jnp.broadcast_to(right, v.shape), pltpu.roll(v, width - 1, 0)
        )
        return before.astype(bf16), after.astype(bf16)

    sides = (0, 1, 4, 5)

    def fill(strips, k, slot, row):
        v = packed[k, slot].astype(f32)
        for j, s in enumerate(sides):
            strips[s, row : row + strip, :] = v[j * strip : (j + 1) * strip]

    def fill_plane(strips, k):
        for m in range(group):
            fill(strips, k, m, height + m * strip)

    def fill_vertical(strips, k):
        fill(strips, k, group, height - strip)
        fill(strips, k, group + 1, 2 * height)

    def fill_halo(strips, g, parts):
        for s in range(2):
            for part in parts:
                k = (2 + s, s, 4 + s)[part]
                v = cols[g, k].astype(f32)
                for j in range(2):
                    strips[4 * s + j, part * height : (part + 1) * height, :] = (
                        v[j * height : (j + 1) * height]
                    )

    def gather(g, strips, im, rows):
        for j in rows:
            v = fields[g, j].astype(f32)
            r = height + j - 2
            strips[2, r : r + 1, :] = v[0:1]
            strips[3, r : r + 1, :] = v[width - 1 : width]
            before, after = shifted(v, strips[1, r : r + 1, :], strips[4, r : r + 1, :])
            im[j * width : (j + 1) * width, 0:ch] = before
            im[j * width : (j + 1) * width, ch : 2 * ch] = after

    every_row = range(height + 4)
    middle_rows = range(2, height + 2)
    outer_rows = (0, 1, height + 2, height + 3)

    def gather_edge(strips, ime, keep):
        for a in range(3):
            for b in range(3):
                lo = height - 2 + a
                lanes = slice((a * 3 + b) * ch, (a * 3 + b + 1) * ch)
                ime[0:pad, lanes] = strips[b, lo : lo + pad, :].astype(bf16)
                ime[pad : 2 * pad, lanes] = strips[3 + b, lo : lo + pad, :].astype(bf16)
        if keep:
            edge[0:pad, :] = strips[1, height - 1 : height - 1 + pad, :]
            edge[pad : 2 * pad, :] = strips[4, height - 1 : height - 1 + pad, :]

    def taps(center, im, ime, blocks):
        for a in range(3):
            for b in range(3):
                pieces = []
                for row, rows in blocks:
                    j = row + a
                    if b == 1:
                        pieces.append(center(j, rows).reshape(rows * width, ch))
                    else:
                        lo = (b // 2) * ch
                        pieces.append(im[j * width : (j + rows) * width, lo : lo + ch])
                if ime is not None:
                    pieces.append(ime[:, (a * 3 + b) * ch : (a * 3 + b + 1) * ch])
                yield jnp.concatenate(pieces, axis=0) if len(pieces) > 1 else pieces[0]

    def kernels(weight, base, lo):
        return [
            weight[a, b * 2 * ch + base : b * 2 * ch + base + ch, lo : lo + ch]
            for a in range(3) for b in range(3)
        ]

    def dot(left, right):
        return jnp.dot(
            jnp.concatenate(left, axis=1), jnp.concatenate(right, axis=0),
            preferred_element_type=f32,
        )

    def x_taps(f, ime, blocks):
        g = first_x + f
        return list(taps(lambda j, rows: fields[g, j : j + rows], im_x, ime, blocks))

    def h_taps(f, ime, blocks):
        return list(taps(lambda j, rows: fields[f, j : j + rows], im_h, ime, blocks))

    whole_ring = ((0, height + 2),)
    whole_tile = ((1, height),)
    inside = ((2, height - 2),)
    ring_rest = ((0, 2), (height, 2))
    tile_rest = ((1, 1), (height, 1))
    bias = lambda n: bias_ref[:, n * ch : (n + 1) * ch]
    last = tile - width

    def store_inside(tile_ref, ring_ref, v, u):
        tile_ref[width:last, :] = v
        if ring_ref is not None:
            ring_ref[2 * width : ring - 2 * width, :] = u

    def store_tile_rest(ref, v):
        ref[0:width, :] = v[0:width]
        ref[last:tile, :] = v[width : 2 * width]

    def store_ring_rest(ref, v):
        ref[0 : 2 * width, :] = v[0 : 2 * width]
        ref[ring - 2 * width : ring + 2 * pad, :] = v[2 * width :]

    def beside(one_side, other_side):
        return [jnp.concatenate(pair, axis=1) for pair in zip(one_side, other_side)]

    def gates(base):
        return [
            wg[a, b * 2 * ch + base : b * 2 * ch + base + ch, :]
            for a in range(3) for b in range(3)
        ]

    def input_part(f):
        gather(first_x + f, strips_x, im_x, every_row)
        gather_edge(strips_x, ime_x, False)
        rx[...] = dot(x_taps(f, ime_x, whole_ring), kernels(wg, 0, ch)) + bias(1)
        v = dot(x_taps(f, None, whole_tile), beside(kernels(wg, 0, 0), kernels(wc, 0, 0)))
        ux[...] = v[:, 0:ch] + bias(0)
        cx[...] = v[:, ch : 2 * ch] + bias(2)

    def passed_input_part(f):
        g = first_x + f
        pass_copy(f).wait_recv()
        wait_sides(g)
        fill_halo(strips_x, g, (1,))
        gather(g, strips_x, im_x, middle_rows)
        v = dot(x_taps(f, None, inside), beside(gates(0), kernels(wc, 0, 0)))
        store_inside(ux, rx, v[:, 0:ch] + bias(0), v[:, ch : 2 * ch] + bias(1))
        store_inside(cx, None, v[:, 2 * ch : 3 * ch] + bias(2), None)
        wait_rows(g)
        fill_halo(strips_x, g, (0, 2))
        gather(g, strips_x, im_x, outer_rows)
        gather_edge(strips_x, ime_x, False)
        store_ring_rest(rx, dot(x_taps(f, ime_x, ring_rest), kernels(wg, 0, ch)) + bias(1))
        v = dot(x_taps(f, None, tile_rest), beside(kernels(wg, 0, 0), kernels(wc, 0, 0)))
        store_tile_rest(ux, v[:, 0:ch] + bias(0))
        store_tile_rest(cx, v[:, ch : 2 * ch] + bias(2))

    def first_state_part():
        gather(0, strips_h, im_h, every_row)
        gather_edge(strips_h, ime_h, True)
        rh[...] = dot(h_taps(0, ime_h, whole_ring), kernels(wg, ch, ch))
        uh[...] = dot(h_taps(0, None, whole_tile), kernels(wg, ch, 0))

    def state_part(f):
        wait_sides(f)
        fill_halo(strips_h, f, (1,))
        gather(f, strips_h, im_h, middle_rows)
        v = dot(h_taps(f, None, inside), gates(ch))
        store_inside(uh, rh, v[:, 0:ch], v[:, ch : 2 * ch])
        wait_rows(f)
        send_out(f - 1)
        fill_halo(strips_h, f, (0, 2))
        gather(f, strips_h, im_h, outer_rows)
        gather_edge(strips_h, ime_h, True)
        store_ring_rest(rh, dot(h_taps(f, ime_h, ring_rest), kernels(wg, ch, ch)))
        store_tile_rest(uh, dot(h_taps(f, None, tile_rest), kernels(wg, ch, 0)))

    def first_part():
        wait_plane(0, True)
        relay(0)
        wait_plane(1, False)
        relay(1)
        fill_plane(strips_h, 0)
        gather(0, strips_h, im_h, middle_rows)
        fill_plane(strips_x, 1)
        gather(first_x, strips_x, im_x, middle_rows)
        copy_wg.wait()
        copy_wc.wait()
        uh[...] = jnp.zeros_like(uh)
        rh[...] = jnp.zeros_like(rh)
        x, h = x_taps(0, None, inside), h_taps(0, None, inside)
        v = dot(x + h, gates(0) + gates(ch))
        store_inside(ux, rx, v[:, 0:ch] + bias(0), v[:, ch : 2 * ch] + bias(1))
        store_inside(cx, None, dot(x, kernels(wc, 0, 0)) + bias(2), None)
        if frame_count > 1:
            wait_plane(2, False)
            relay(2)
        wait_vertical(0)
        fill_vertical(strips_h, 0)
        gather(0, strips_h, im_h, outer_rows)
        gather_edge(strips_h, ime_h, True)
        wait_vertical(1)
        fill_vertical(strips_x, 1)
        gather(first_x, strips_x, im_x, outer_rows)
        gather_edge(strips_x, ime_x, False)
        x, h = x_taps(0, ime_x, ring_rest), h_taps(0, ime_h, ring_rest)
        store_ring_rest(rx, dot(x + h, kernels(wg, 0, ch) + kernels(wg, ch, ch)) + bias(1))
        x, h = x_taps(0, None, tile_rest), h_taps(0, None, tile_rest)
        store_tile_rest(ux, dot(x + h, kernels(wg, 0, 0) + kernels(wg, ch, 0)) + bias(0))
        store_tile_rest(cx, dot(x, kernels(wc, 0, 0)) + bias(2))

    def update_state(f):
        rs_edge[...] = sigmoid(rx[ring:, :] + rh[ring:, :]) * edge[...]
        for j in range(height + 2):
            rows = slice(j * width, (j + 1) * width)
            v = sigmoid(rx[rows, :] + rh[rows, :]) * fields[f, 1 + j].astype(f32)
            rs[j] = v.astype(bf16)
            before, after = shifted(v, rs_edge[j : j + 1, :], rs_edge[pad + j : pad + j + 1, :])
            im_rs[rows, 0:ch] = before
            im_rs[rows, ch : 2 * ch] = after
        summed = dot(
            list(taps(lambda j, rows: rs[j : j + rows], im_rs, None, ((0, height),))),
            kernels(wc, ch, 0),
        )
        for i in range(height):
            rows = slice(i * width, (i + 1) * width)
            update = sigmoid(ux[rows, :] + uh[rows, :])
            candidate = jnp.tanh(cx[rows, :] + summed[rows])
            fresh = (1.0 - update) * fields[f, 2 + i].astype(f32) + update * candidate
            fields[f + 1, 2 + i] = fresh.astype(bf16)
            stage_row(i, fresh)
        stage[f + 1] = stage32[...].astype(bf16)

    place_own().wait()
    pl.when(layer == 0)(first_part)

    @pl.when(layer > 0)
    def _():
        wait_plane(0, True)
        relay(0)
        wait_vertical(0)
        fill_plane(strips_h, 0)
        fill_vertical(strips_h, 0)
        copy_wg.wait()
        copy_wc.wait()
        first_state_part()

    def step(f, carry):
        @pl.when(layer > 0)
        def _():
            passed_input_part(f)

        @pl.when(f > 0)
        def _():
            state_part(f)

        update_state(f)
        more, onward = f + 1 < frame_count, layer < last_layer
        pl.when(more)(lambda: send_halo(f + 1, f + 1, 0, side_dirs))
        pl.when(onward)(lambda: send_halo(f + 1, first_x + f, 1, side_dirs))
        pl.when(more)(lambda: send_halo(f + 1, f + 1, 0, other_dirs))

        @pl.when(onward)
        def _():
            pass_copy(f).start()
            send_halo(f + 1, first_x + f, 1, other_dirs)

        @pl.when(both(layer == 0, f + 2 < frame_count))
        def _():
            wait_plane(f + 3, False)
            relay(f + 3)

        @pl.when(both(layer == 0, f + 1 < frame_count))
        def _():
            wait_vertical(f + 2)
            fill_plane(strips_x, f + 2)
            fill_vertical(strips_x, f + 2)
            input_part(f + 1)

        return carry

    lax.fori_loop(0, frame_count, step, 0)
    send_out(frame_count - 1)

    sent_relay(0)

    @pl.when(layer < last_layer)
    def _():
        sent_push(0, True)
        for k in range(1, 1 + frame_count):
            sent_relay(k)

    @pl.when(layer == last_layer)
    def _():
        for k in range(2, 1 + frame_count):
            sent_push(k, False)

    def finish(f, carry):
        pl.when(f + 1 < frame_count)(lambda: sent_halo(f + 1, 0))

        @pl.when(layer < last_layer)
        def _():
            pass_copy(f).wait_send()
            sent_halo(f + 1, 1)

        own_out(f).wait()
        drain((group - 1) * strip * width, send_sem=out_send.at[f])
        drain((group - 1) * strip * width, recv_sem=out_recv.at[f])
        return carry

    lax.fori_loop(0, frame_count, finish, 0)


def shards(count, frames, initial_state, w_gates, w_cand, biases):
    frame_count, strip, cols, ch = frames.shape
    group = 4 if count % 4 == 0 else 1
    height, width = strip * group, cols // group
    dma = pltpu.SemaphoreType.DMA
    bf16, f32 = jnp.bfloat16, jnp.float32
    anywhere = pl.BlockSpec(memory_space=pltpu.HBM)
    rows_k = w_gates.shape[2] * w_gates.shape[3]
    tile = height * width
    ring = (height + 2) * width
    pad = -(-(height + 2) // 16) * 16
    pack_rows = -(-4 * strip // 16) * 16
    held = 2 * frame_count + 1
    out = (1, frame_count, strip, cols, ch)
    return pl.pallas_call(
        functools.partial(kernel, count, group),
        out_shape=pltpu.VMEM(out, bf16),
        in_specs=[anywhere] * 4 + [pl.BlockSpec(memory_space=pltpu.VMEM)],
        out_specs=pl.BlockSpec(memory_space=pltpu.VMEM),
        scratch_shapes=[
            pltpu.VMEM((3, rows_k, 2 * ch), bf16),
            pltpu.VMEM((3, rows_k, ch), bf16),
            pltpu.VMEM((1 + frame_count, strip, cols, ch), bf16),
            pltpu.VMEM((1 + frame_count, group, pack_rows, ch), bf16),
            pltpu.VMEM((group, pack_rows, ch), f32),
            pltpu.VMEM((1 + frame_count, group + 2, pack_rows, ch), bf16),
            pltpu.VMEM((held, height + 4, width, ch), bf16),
            pltpu.VMEM((held, 6, 2 * height, ch), bf16),
            pltpu.VMEM((frame_count + 1, 2, 2 * height, ch), bf16),
            pltpu.VMEM((2, 2 * height, ch), f32),
            pltpu.VMEM((6, 3 * height, ch), f32),
            pltpu.VMEM((6, 3 * height, ch), f32),
            pltpu.VMEM(((height + 4) * width, 2 * ch), bf16),
            pltpu.VMEM((2 * pad, 9 * ch), bf16),
            pltpu.VMEM(((height + 4) * width, 2 * ch), bf16),
            pltpu.VMEM((2 * pad, 9 * ch), bf16),
            pltpu.VMEM((2 * pad, ch), f32),
            pltpu.VMEM((ring + 2 * pad, ch), f32),
            pltpu.VMEM((tile, ch), f32),
            pltpu.VMEM((tile, ch), f32),
            pltpu.VMEM((ring + 2 * pad, ch), f32),
            pltpu.VMEM((tile, ch), f32),
            pltpu.VMEM((height + 2, width, ch), bf16),
            pltpu.VMEM((ring, 2 * ch), bf16),
            pltpu.VMEM((2 * pad, ch), f32),
            pltpu.VMEM((group * (strip * width + pack_rows), ch), bf16),
            dma((2,)), dma((2 + frame_count,)),
            dma((2, 1 + frame_count)), dma((2, 1 + frame_count)),
            dma((frame_count,)), dma((frame_count,)),
            dma((frame_count,)), dma((frame_count,)), dma((frame_count,)),
            dma((2, frame_count + 1)), dma((2, held)),
        ],
        compiler_params=pltpu.CompilerParams(
            collective_id=0, has_side_effects=True, vmem_limit_bytes=60_000_000
        ),
    )(
        frames,
        initial_state[0],
        w_gates.reshape(3, rows_k, 2 * ch),
        w_cand.reshape(3, rows_k, ch),
        biases,
    )


def solution(mesh):
    placed = (
        P(None, "rows", None, None),
        P("layer", "rows", None, None),
        P("layer", None, None, None, None),
        P("layer", None, None, None, None),
        P("layer", None),
    )
    return jax.shard_map(
        functools.partial(shards, mesh.shape["rows"]),
        mesh=mesh,
        in_specs=placed,
        out_specs=P("layer", None, "rows", None, None),
        check_vma=False,
    )
```

```python
import functools

import jax
import jax.numpy as jnp
from jax import lax
from jax.experimental import pallas as pl
from jax.experimental.pallas import tpu as pltpu
from jax.sharding import PartitionSpec as P

MESH = pl.DeviceIdType.MESH

ROW_DIRS = ((-1, 0), (1, 0))
COL_DIRS = ((0, -1), (0, 1), (-1, -1), (-1, 1), (1, -1), (1, 1))
DIRS = ROW_DIRS + COL_DIRS


def reorder(c, group):
    if group == 4:
        return c + (c // 2) * (5 - 2 * c)
    return c


def sigmoid(v):
    return 0.5 * jnp.tanh(0.5 * v) + 0.5


def kernel(
    count, group, frames_ref, init_ref, wg_ref, wc_ref, bias_ref, out_ref,
    wg, wc, own, packs, packs32, packed, fields, cols, stage, stage32,
    strips_x, strips_h, im_x, ime_x, im_h, ime_h, edge,
    rx, ux, cx, rh, uh, rs, im_rs, rs_edge, span,
    w_sem, load_sem, push_send, push_recv, pass_send, pass_recv,
    out_own, out_send, out_recv, halo_send, halo_recv,
):
    frame_count, strip, all_cols, ch = frames_ref.shape
    height = strip * group
    width = all_cols // group
    tile = height * width
    ring = (height + 2) * width
    pad = ime_x.shape[0] // 2
    layer = lax.axis_index("layer")
    last_layer = lax.axis_size("layer") - 1
    index = lax.axis_index("rows")
    planes = count // group
    q = index // group
    c = index % group
    t = reorder(c, group)
    first_x = frame_count + 1
    f32, bf16 = jnp.float32, jnp.bfloat16
    both = jnp.logical_and
    one = lambda cond: jnp.where(cond, 1, 0)

    def exists(step_row, step_col):
        terms = []
        if step_row < 0:
            terms.append(q > 0)
        if step_row > 0:
            terms.append(q < planes - 1)
        if step_col < 0:
            terms.append(t > 0)
        if step_col > 0:
            terms.append(t < group - 1)
        return functools.reduce(jnp.logical_and, terms)

    def at(step_row, step_col, hop=0):
        rows = (q + step_row) * group + reorder(t + step_col, group)
        return {"layer": layer + hop, "rows": rows}

    def member(d):
        return lax.rem(c + d, group)

    def others():
        if group == 4:
            return [3 - c, c + 2 - 4 * (c // 2), c + 1 - 2 * (c % 2)]
        return [member(d) for d in range(1, group)]

    def send(src, dst, send_sem, recv_sem, where):
        return pltpu.make_async_remote_copy(
            src_ref=src, dst_ref=dst, send_sem=send_sem, recv_sem=recv_sem,
            device_id=where, device_id_type=MESH,
        )

    def drain(pixels, send_sem=None, recv_sem=None):
        part = span.at[pl.ds(0, pixels)]
        sem = recv_sem if send_sem is None else send_sem
        copy = send(part, part, sem, sem, {"layer": last_layer - layer})
        copy.wait_recv() if send_sem is None else copy.wait_send()

    copy_wg = pltpu.make_async_copy(wg_ref, wg, w_sem.at[0])
    copy_wc = pltpu.make_async_copy(wc_ref, wc, w_sem.at[1])
    own_cols = pl.ds(pl.multiple_of(t * width, width), width)
    own_rows = pl.ds(2 + c * strip, strip)
    inner = pl.ds(2, height)
    above, below = pl.ds(0, 2), pl.ds(height + 2, 2)

    def load(k):
        src = init_ref if k == 0 else frames_ref.at[k - 1]
        return pltpu.make_async_copy(src, own.at[k], load_sem.at[k])

    def place_own():
        return pltpu.make_async_copy(
            own.at[0, :, own_cols, :], fields.at[0, own_rows], load_sem.at[1 + frame_count]
        )

    def push(k, to_layer, skip_self):
        g = 0 if k == 0 else first_x + k - 1
        for target in others() if skip_self else others() + [c]:
            place = reorder(target, group)
            tcols = pl.ds(pl.multiple_of(place * width, width), width)
            where = {"layer": to_layer, "rows": q * group + target}
            sems = push_send.at[0, k], push_recv.at[0, k]
            send(own.at[k, :, tcols, :], fields.at[g, own_rows], *sems, where).start()
            send(packs.at[k, place], packed.at[k, c], *sems, where).start()

    pack_rows = packs.shape[2]
    pushed = strip * width + pack_rows

    def relay(k):
        g = 0 if isinstance(k, int) and k == 0 else first_x + k - 1
        for step, src, dst, sent, slot in (
            (-1, pl.ds(2, 2), below, 0, group + 1),
            (1, pl.ds(height, 2), above, group - 1, group),
        ):
            @pl.when(exists(step, 0))
            def _(step=step, src=src, dst=dst, sent=sent, slot=slot):
                sems = push_send.at[1, k], push_recv.at[1, k]
                where = at(step, 0)
                send(fields.at[g, src], fields.at[g, dst], *sems, where).start()
                send(packed.at[k, sent], packed.at[k, slot], *sems, where).start()

    def sent_push(k, skip_self):
        drain((group - 1 if skip_self else group) * pushed, send_sem=push_send.at[0, k])

    def sent_relay(k):
        for n in (1, 2):
            @pl.when(one(q > 0) + one(q < planes - 1) == n)
            def _(n=n):
                drain(n * pushed, send_sem=push_send.at[1, k])

    def wait_plane(k, skip_self):
        drain((group - 1 if skip_self else group) * pushed, recv_sem=push_recv.at[0, k])

    def wait_vertical(k):
        for n in (1, 2):
            @pl.when(one(q > 0) + one(q < planes - 1) == n)
            def _(n=n):
                drain(n * pushed, recv_sem=push_recv.at[1, k])

    def pass_copy(f):
        return send(
            fields.at[f + 1, inner], fields.at[first_x + f, inner],
            pass_send.at[f], pass_recv.at[f], {"layer": jnp.minimum(layer + 1, last_layer)},
        )

    def own_out(f):
        return pltpu.make_async_copy(
            fields.at[f + 1, own_rows], out_ref.at[0, f, :, own_cols, :], out_own.at[f]
        )

    def send_out(f):
        for target in others():
            send(
                fields.at[f + 1, pl.ds(2 + target * strip, strip)],
                out_ref.at[0, f, :, own_cols, :],
                out_send.at[f], out_recv.at[f], {"rows": q * group + target},
            ).start()
        own_out(f).start()

    def halo_copy(src, dst, k, hop):
        dr, dc = DIRS[k]
        back = DIRS.index((-dr, -dc))
        if dc == 0:
            src_ref = fields.at[src, pl.ds(2, 2) if dr < 0 else pl.ds(height, 2)]
            dst_ref = fields.at[dst, below if dr < 0 else above]
        else:
            src_ref = stage.at[src, 0 if dc < 0 else 1]
            dst_ref = cols.at[dst, back - 2]
        kind = 0 if dr == 0 else 1
        return send(
            src_ref, dst_ref, halo_send.at[hop, src], halo_recv.at[kind, dst], at(dr, dc, hop)
        )

    side_dirs, other_dirs = (2, 3), (4, 5, 6, 7, 0, 1)

    def send_halo(src, dst, hop, dirs):
        for k in dirs:
            pl.when(exists(*DIRS[k]))(lambda k=k: halo_copy(src, dst, k, hop).start())

    upright = one(q > 0) + one(q < planes - 1)
    sideways = one(t > 0) + one(t < group - 1)
    uprights = (1, 2) if planes > 1 else (0,)
    side_pixels, row_pixels = 2 * height, 2 * width

    def sent_halo(src, hop):
        for u in uprights:
            for v in (1, 2):
                @pl.when(both(upright == u, sideways == v))
                def _(u=u, v=v):
                    pixels = u * row_pixels + v * (1 + u) * side_pixels
                    drain(pixels, send_sem=halo_send.at[hop, src])

    def wait_sides(dst):
        for v in (1, 2):
            @pl.when(sideways == v)
            def _(v=v):
                drain(v * side_pixels, recv_sem=halo_recv.at[0, dst])

    def wait_rows(dst):
        for u in uprights:
            for v in (1, 2):
                if u:
                    @pl.when(both(upright == u, sideways == v))
                    def _(u=u, v=v):
                        drain(u * (row_pixels + v * side_pixels), recv_sem=halo_recv.at[1, dst])

    load(0).start()

    @pl.when(layer == last_layer)
    def _():
        for k in range(1, 1 + frame_count):
            load(k).start()

    copy_wg.start()
    copy_wc.start()

    barrier = pltpu.get_barrier_semaphore()
    expected = (group - 1) + group * last_layer
    for hop in range(2):
        where_layer = layer if hop == 0 else last_layer - layer
        for d in range(0 if hop else 1, group):
            pl.semaphore_signal(
                barrier, inc=1, device_id={"layer": where_layer, "rows": q * group + member(d)},
                device_id_type=MESH,
            )
        for dr, dc in DIRS:
            if dr != 0:
                @pl.when(exists(dr, dc))
                def _(dr=dr, dc=dc, where_layer=where_layer):
                    where = {"layer": where_layer, "rows": at(dr, dc)["rows"]}
                    pl.semaphore_signal(barrier, inc=1, device_id=where, device_id_type=MESH)

                expected = expected + one(exists(dr, dc))

    for dr, dc in ROW_DIRS:
        @pl.when(jnp.logical_not(exists(dr, dc)))
        def _(dr=dr):
            def clear(g, carry):
                fields[g, above if dr < 0 else below] = jnp.zeros((2, width, ch), bf16)
                return carry

            lax.fori_loop(0, 2 * frame_count + 1, clear, 0)
            for k in range(1 + frame_count):
                packed[k, group if dr < 0 else group + 1] = jnp.zeros((pack_rows, ch), bf16)

    for k, (dr, dc) in enumerate(COL_DIRS):
        @pl.when(jnp.logical_not(exists(dr, dc)))
        def _(k=k):
            def clear(g, carry):
                cols[g, k] = jnp.zeros((2 * height, ch), bf16)
                return carry

            lax.fori_loop(1, 2 * frame_count + 1, clear, 0)

    strips_x[...] = jnp.zeros_like(strips_x)
    strips_h[...] = jnp.zeros_like(strips_h)
    packs32[...] = jnp.zeros_like(packs32)

    def make_packs(k):
        for place in range(group):
            for r in range(strip):
                lo, hi = place * width, (place + 1) * width
                if place > 0:
                    v = own[k, r, lo - 16 : lo, :].astype(f32)
                    packs32[place, r : r + 1, :] = v[14:15]
                    packs32[place, strip + r : strip + r + 1, :] = v[15:16]
                if place < group - 1:
                    v = own[k, r, hi : hi + 16, :].astype(f32)
                    packs32[place, 2 * strip + r : 2 * strip + r + 1, :] = v[0:1]
                    packs32[place, 3 * strip + r : 3 * strip + r + 1, :] = v[1:2]
        packs[k] = packs32[...].astype(bf16)

    @pl.when(layer == last_layer)
    def _():
        load(1).wait()
        make_packs(1)

    @pl.when(layer < last_layer)
    def _():
        load(0).wait()
        make_packs(0)

    pl.semaphore_wait(barrier, expected)

    @pl.when(layer < last_layer)
    def _():
        push(0, layer, True)

    @pl.when(layer == last_layer)
    def _():
        push(1, 0, False)
        load(0).wait()
        make_packs(0)
        for k in range(2, 1 + frame_count):
            load(k).wait()
            make_packs(k)
        sent_push(1, False)
        push(0, layer, True)
        sent_push(0, True)
        for k in range(2, 1 + frame_count):
            push(k, 0, False)

    packed[0, c] = packs[0, t]
    place_own().start()

    first_col = lax.broadcasted_iota(jnp.int32, (width, ch), 0) == 0
    last_col = lax.broadcasted_iota(jnp.int32, (width, ch), 0) == width - 1

    def stage_row(i, v):
        for s, lo in enumerate((0, width - 2)):
            for k in range(2):
                stage32[s, k * height + i : k * height + i + 1, :] = v[lo + k : lo + k + 1]

    def shifted(v, left, right):
        before = jnp.where(first_col, jnp.broadcast_to(left, v.shape), pltpu.roll(v, 1, 0))
        after = jnp.where(
            last_col, jnp.broadcast_to(right, v.shape), pltpu.roll(v, width - 1, 0)
        )
        return before.astype(bf16), after.astype(bf16)

    sides = (0, 1, 4, 5)

    def fill(strips, k, slot, row):
        v = packed[k, slot].astype(f32)
        for j, s in enumerate(sides):
            strips[s, row : row + strip, :] = v[j * strip : (j + 1) * strip]

    def fill_plane(strips, k):
        for m in range(group):
            fill(strips, k, m, height + m * strip)

    def fill_vertical(strips, k):
        fill(strips, k, group, height - strip)
        fill(strips, k, group + 1, 2 * height)

    def fill_halo(strips, g, parts):
        for s in range(2):
            for part in parts:
                k = (2 + s, s, 4 + s)[part]
                v = cols[g, k].astype(f32)
                for j in range(2):
                    strips[4 * s + j, part * height : (part + 1) * height, :] = (
                        v[j * height : (j + 1) * height]
                    )

    def gather(g, strips, im, rows):
        for j in rows:
            v = fields[g, j].astype(f32)
            r = height + j - 2
            strips[2, r : r + 1, :] = v[0:1]
            strips[3, r : r + 1, :] = v[width - 1 : width]
            before, after = shifted(v, strips[1, r : r + 1, :], strips[4, r : r + 1, :])
            im[j * width : (j + 1) * width, 0:ch] = before
            im[j * width : (j + 1) * width, ch : 2 * ch] = after

    every_row = range(height + 4)
    middle_rows = range(2, height + 2)
    outer_rows = (0, 1, height + 2, height + 3)

    def gather_edge(strips, ime, keep):
        for a in range(3):
            for b in range(3):
                lo = height - 2 + a
                lanes = slice((a * 3 + b) * ch, (a * 3 + b + 1) * ch)
                ime[0:pad, lanes] = strips[b, lo : lo + pad, :].astype(bf16)
                ime[pad : 2 * pad, lanes] = strips[3 + b, lo : lo + pad, :].astype(bf16)
        if keep:
            edge[0:pad, :] = strips[1, height - 1 : height - 1 + pad, :]
            edge[pad : 2 * pad, :] = strips[4, height - 1 : height - 1 + pad, :]

    def taps(center, im, ime, blocks):
        for a in range(3):
            for b in range(3):
                pieces = []
                for row, rows in blocks:
                    j = row + a
                    if b == 1:
                        pieces.append(center(j, rows).reshape(rows * width, ch))
                    else:
                        lo = (b // 2) * ch
                        pieces.append(im[j * width : (j + rows) * width, lo : lo + ch])
                if ime is not None:
                    pieces.append(ime[:, (a * 3 + b) * ch : (a * 3 + b + 1) * ch])
                yield jnp.concatenate(pieces, axis=0) if len(pieces) > 1 else pieces[0]

    def kernels(weight, base, lo):
        return [
            weight[a, b * 2 * ch + base : b * 2 * ch + base + ch, lo : lo + ch]
            for a in range(3) for b in range(3)
        ]

    def dot(left, right):
        return jnp.dot(
            jnp.concatenate(left, axis=1), jnp.concatenate(right, axis=0),
            preferred_element_type=f32,
        )

    def x_taps(f, ime, blocks):
        g = first_x + f
        return list(taps(lambda j, rows: fields[g, j : j + rows], im_x, ime, blocks))

    def h_taps(f, ime, blocks):
        return list(taps(lambda j, rows: fields[f, j : j + rows], im_h, ime, blocks))

    whole_ring = ((0, height + 2),)
    whole_tile = ((1, height),)
    inside = ((2, height - 2),)
    ring_rest = ((0, 2), (height, 2))
    tile_rest = ((1, 1), (height, 1))
    bias = lambda n: bias_ref[:, n * ch : (n + 1) * ch]
    last = tile - width

    def store_inside(tile_ref, ring_ref, v, u):
        tile_ref[width:last, :] = v
        if ring_ref is not None:
            ring_ref[2 * width : ring - 2 * width, :] = u

    def store_tile_rest(ref, v):
        ref[0:width, :] = v[0:width]
        ref[last:tile, :] = v[width : 2 * width]

    def store_ring_rest(ref, v):
        ref[0 : 2 * width, :] = v[0 : 2 * width]
        ref[ring - 2 * width : ring + 2 * pad, :] = v[2 * width :]

    def beside(one_side, other_side):
        return [jnp.concatenate(pair, axis=1) for pair in zip(one_side, other_side)]

    def gates(base):
        return [
            wg[a, b * 2 * ch + base : b * 2 * ch + base + ch, :]
            for a in range(3) for b in range(3)
        ]

    def input_part(f):
        gather(first_x + f, strips_x, im_x, every_row)
        gather_edge(strips_x, ime_x, False)
        rx[...] = dot(x_taps(f, ime_x, whole_ring), kernels(wg, 0, ch)) + bias(1)
        v = dot(x_taps(f, None, whole_tile), beside(kernels(wg, 0, 0), kernels(wc, 0, 0)))
        ux[...] = v[:, 0:ch] + bias(0)
        cx[...] = v[:, ch : 2 * ch] + bias(2)

    def passed_input_part(f):
        g = first_x + f
        pass_copy(f).wait_recv()
        wait_sides(g)
        fill_halo(strips_x, g, (1,))
        gather(g, strips_x, im_x, middle_rows)
        v = dot(x_taps(f, None, inside), beside(gates(0), kernels(wc, 0, 0)))
        store_inside(ux, rx, v[:, 0:ch] + bias(0), v[:, ch : 2 * ch] + bias(1))
        store_inside(cx, None, v[:, 2 * ch : 3 * ch] + bias(2), None)
        wait_rows(g)
        fill_halo(strips_x, g, (0, 2))
        gather(g, strips_x, im_x, outer_rows)
        gather_edge(strips_x, ime_x, False)
        store_ring_rest(rx, dot(x_taps(f, ime_x, ring_rest), kernels(wg, 0, ch)) + bias(1))
        v = dot(x_taps(f, None, tile_rest), beside(kernels(wg, 0, 0), kernels(wc, 0, 0)))
        store_tile_rest(ux, v[:, 0:ch] + bias(0))
        store_tile_rest(cx, v[:, ch : 2 * ch] + bias(2))

    def first_state_part():
        gather(0, strips_h, im_h, every_row)
        gather_edge(strips_h, ime_h, True)
        rh[...] = dot(h_taps(0, ime_h, whole_ring), kernels(wg, ch, ch))
        uh[...] = dot(h_taps(0, None, whole_tile), kernels(wg, ch, 0))

    def state_part(f):
        wait_sides(f)
        fill_halo(strips_h, f, (1,))
        gather(f, strips_h, im_h, middle_rows)
        v = dot(h_taps(f, None, inside), gates(ch))
        store_inside(uh, rh, v[:, 0:ch], v[:, ch : 2 * ch])
        wait_rows(f)
        send_out(f - 1)
        fill_halo(strips_h, f, (0, 2))
        gather(f, strips_h, im_h, outer_rows)
        gather_edge(strips_h, ime_h, True)
        store_ring_rest(rh, dot(h_taps(f, ime_h, ring_rest), kernels(wg, ch, ch)))
        store_tile_rest(uh, dot(h_taps(f, None, tile_rest), kernels(wg, ch, 0)))

    def first_part():
        wait_plane(0, True)
        relay(0)
        wait_plane(1, False)
        relay(1)
        fill_plane(strips_h, 0)
        gather(0, strips_h, im_h, middle_rows)
        fill_plane(strips_x, 1)
        gather(first_x, strips_x, im_x, middle_rows)
        copy_wg.wait()
        copy_wc.wait()
        uh[...] = jnp.zeros_like(uh)
        rh[...] = jnp.zeros_like(rh)
        x, h = x_taps(0, None, inside), h_taps(0, None, inside)
        v = dot(x + h, gates(0) + gates(ch))
        store_inside(ux, rx, v[:, 0:ch] + bias(0), v[:, ch : 2 * ch] + bias(1))
        store_inside(cx, None, dot(x, kernels(wc, 0, 0)) + bias(2), None)
        if frame_count > 1:
            wait_plane(2, False)
            relay(2)
        wait_vertical(0)
        fill_vertical(strips_h, 0)
        gather(0, strips_h, im_h, outer_rows)
        gather_edge(strips_h, ime_h, True)
        wait_vertical(1)
        fill_vertical(strips_x, 1)
        gather(first_x, strips_x, im_x, outer_rows)
        gather_edge(strips_x, ime_x, False)
        x, h = x_taps(0, ime_x, ring_rest), h_taps(0, ime_h, ring_rest)
        store_ring_rest(rx, dot(x + h, kernels(wg, 0, ch) + kernels(wg, ch, ch)) + bias(1))
        x, h = x_taps(0, None, tile_rest), h_taps(0, None, tile_rest)
        store_tile_rest(ux, dot(x + h, kernels(wg, 0, 0) + kernels(wg, ch, 0)) + bias(0))
        store_tile_rest(cx, dot(x, kernels(wc, 0, 0)) + bias(2))

    def update_state(f):
        rs_edge[...] = sigmoid(rx[ring:, :] + rh[ring:, :]) * edge[...]
        for j in range(height + 2):
            rows = slice(j * width, (j + 1) * width)
            v = sigmoid(rx[rows, :] + rh[rows, :]) * fields[f, 1 + j].astype(f32)
            rs[j] = v.astype(bf16)
            before, after = shifted(v, rs_edge[j : j + 1, :], rs_edge[pad + j : pad + j + 1, :])
            im_rs[rows, 0:ch] = before
            im_rs[rows, ch : 2 * ch] = after
        summed = dot(
            list(taps(lambda j, rows: rs[j : j + rows], im_rs, None, ((0, height),))),
            kernels(wc, ch, 0),
        )
        for i in range(height):
            rows = slice(i * width, (i + 1) * width)
            update = sigmoid(ux[rows, :] + uh[rows, :])
            candidate = jnp.tanh(cx[rows, :] + summed[rows])
            fresh = (1.0 - update) * fields[f, 2 + i].astype(f32) + update * candidate
            fields[f + 1, 2 + i] = fresh.astype(bf16)
            stage_row(i, fresh)
        stage[f + 1] = stage32[...].astype(bf16)

    place_own().wait()
    pl.when(layer == 0)(first_part)

    @pl.when(layer > 0)
    def _():
        wait_plane(0, True)
        relay(0)
        wait_vertical(0)
        fill_plane(strips_h, 0)
        fill_vertical(strips_h, 0)
        copy_wg.wait()
        copy_wc.wait()
        first_state_part()

    def step(f, carry):
        @pl.when(layer > 0)
        def _():
            passed_input_part(f)

        @pl.when(f > 0)
        def _():
            state_part(f)

        update_state(f)
        more, onward = f + 1 < frame_count, layer < last_layer
        pl.when(more)(lambda: send_halo(f + 1, f + 1, 0, side_dirs))
        pl.when(more)(lambda: send_halo(f + 1, f + 1, 0, other_dirs))
        pl.when(onward)(lambda: send_halo(f + 1, first_x + f, 1, side_dirs))

        @pl.when(onward)
        def _():
            send_halo(f + 1, first_x + f, 1, other_dirs)
            pass_copy(f).start()

        @pl.when(both(layer == 0, f + 2 < frame_count))
        def _():
            wait_plane(f + 3, False)
            relay(f + 3)

        @pl.when(both(layer == 0, f + 1 < frame_count))
        def _():
            wait_vertical(f + 2)
            fill_plane(strips_x, f + 2)
            fill_vertical(strips_x, f + 2)
            input_part(f + 1)

        return carry

    lax.fori_loop(0, frame_count, step, 0)
    send_out(frame_count - 1)

    sent_relay(0)

    @pl.when(layer < last_layer)
    def _():
        sent_push(0, True)
        for k in range(1, 1 + frame_count):
            sent_relay(k)

    @pl.when(layer == last_layer)
    def _():
        for k in range(2, 1 + frame_count):
            sent_push(k, False)

    def finish(f, carry):
        pl.when(f + 1 < frame_count)(lambda: sent_halo(f + 1, 0))

        @pl.when(layer < last_layer)
        def _():
            pass_copy(f).wait_send()
            sent_halo(f + 1, 1)

        own_out(f).wait()
        drain((group - 1) * strip * width, send_sem=out_send.at[f])
        drain((group - 1) * strip * width, recv_sem=out_recv.at[f])
        return carry

    lax.fori_loop(0, frame_count, finish, 0)


def shards(count, frames, initial_state, w_gates, w_cand, biases):
    frame_count, strip, cols, ch = frames.shape
    group = 4 if count % 4 == 0 else 1
    height, width = strip * group, cols // group
    dma = pltpu.SemaphoreType.DMA
    bf16, f32 = jnp.bfloat16, jnp.float32
    anywhere = pl.BlockSpec(memory_space=pltpu.HBM)
    rows_k = w_gates.shape[2] * w_gates.shape[3]
    tile = height * width
    ring = (height + 2) * width
    pad = -(-(height + 2) // 16) * 16
    pack_rows = -(-4 * strip // 16) * 16
    held = 2 * frame_count + 1
    out = (1, frame_count, strip, cols, ch)
    return pl.pallas_call(
        functools.partial(kernel, count, group),
        out_shape=pltpu.VMEM(out, bf16),
        in_specs=[anywhere] * 4 + [pl.BlockSpec(memory_space=pltpu.VMEM)],
        out_specs=pl.BlockSpec(memory_space=pltpu.VMEM),
        scratch_shapes=[
            pltpu.VMEM((3, rows_k, 2 * ch), bf16),
            pltpu.VMEM((3, rows_k, ch), bf16),
            pltpu.VMEM((1 + frame_count, strip, cols, ch), bf16),
            pltpu.VMEM((1 + frame_count, group, pack_rows, ch), bf16),
            pltpu.VMEM((group, pack_rows, ch), f32),
            pltpu.VMEM((1 + frame_count, group + 2, pack_rows, ch), bf16),
            pltpu.VMEM((held, height + 4, width, ch), bf16),
            pltpu.VMEM((held, 6, 2 * height, ch), bf16),
            pltpu.VMEM((frame_count + 1, 2, 2 * height, ch), bf16),
            pltpu.VMEM((2, 2 * height, ch), f32),
            pltpu.VMEM((6, 3 * height, ch), f32),
            pltpu.VMEM((6, 3 * height, ch), f32),
            pltpu.VMEM(((height + 4) * width, 2 * ch), bf16),
            pltpu.VMEM((2 * pad, 9 * ch), bf16),
            pltpu.VMEM(((height + 4) * width, 2 * ch), bf16),
            pltpu.VMEM((2 * pad, 9 * ch), bf16),
            pltpu.VMEM((2 * pad, ch), f32),
            pltpu.VMEM((ring + 2 * pad, ch), f32),
            pltpu.VMEM((tile, ch), f32),
            pltpu.VMEM((tile, ch), f32),
            pltpu.VMEM((ring + 2 * pad, ch), f32),
            pltpu.VMEM((tile, ch), f32),
            pltpu.VMEM((height + 2, width, ch), bf16),
            pltpu.VMEM((ring, 2 * ch), bf16),
            pltpu.VMEM((2 * pad, ch), f32),
            pltpu.VMEM((group * (strip * width + pack_rows), ch), bf16),
            dma((2,)), dma((2 + frame_count,)),
            dma((2, 1 + frame_count)), dma((2, 1 + frame_count)),
            dma((frame_count,)), dma((frame_count,)),
            dma((frame_count,)), dma((frame_count,)), dma((frame_count,)),
            dma((2, frame_count + 1)), dma((2, held)),
        ],
        compiler_params=pltpu.CompilerParams(
            collective_id=0, has_side_effects=True, vmem_limit_bytes=60_000_000
        ),
    )(
        frames,
        initial_state[0],
        w_gates.reshape(3, rows_k, 2 * ch),
        w_cand.reshape(3, rows_k, ch),
        biases,
    )


def solution(mesh):
    placed = (
        P(None, "rows", None, None),
        P("layer", "rows", None, None),
        P("layer", None, None, None, None),
        P("layer", None, None, None, None),
        P("layer", None),
    )
    return jax.shard_map(
        functools.partial(shards, mesh.shape["rows"]),
        mesh=mesh,
        in_specs=placed,
        out_specs=P("layer", None, "rows", None, None),
        check_vma=False,
    )
```
